32 devices in a mesh: sec: 2 (over core), cell: 16 (over z, y, x).
Axes of the slice: x: 2, y: 2, z: 4, core: 2. Of those that a mesh axis runs over, the one named last changes fastest.
Arguments:
- elem_disp: float32 [64, 24], P('cell'), may hold values from -0.9 to 0.9
- plastic_strain: float32 [64, 8, 6, 4096], P('cell', 'sec'), may hold values from -0.06 to 0.06
- hardening_var: float32 [64, 8, 4096], P('cell', 'sec'), may hold values from 0 to 0.1
- shear_mod: float32 [64, 8, 4096], P('cell', 'sec'), may hold values from 0.5 to 4
- bulk_mod: float32 [64, 8, 4096], P('cell', 'sec'), may hold values from 1.5 to 8
- yield_stress: float32 [64, 8, 4096], P('cell', 'sec'), may hold values from 0.1 to 0.4
- sat_stress: float32 [64, 8, 4096], P('cell', 'sec'), may hold values from 0.05 to 0.3
- sat_rate: float32 [64, 8, 4096], P('cell', 'sec'), may hold values from 5 to 50
- fft_iters: int32 [64, 8], P('cell', 'sec'), may hold values from 2 to 8, as said below
- rm_iters: int32 [64, 8], P('cell', 'sec'), may hold values from 1 to 3, as said below
- move_flag: int32 [64, 8], P('cell', 'sec'), may hold values from 0 to 1, as said below
Outputs:
- elem_force: float32 [64, 24], P('cell')
- elem_stiff: float32 [64, 576], P('cell')
- point_stress: float32 [64, 8, 6], P('cell', 'sec')
- new_state: float32 [64, 8, 7, 4096], P('cell', 'sec')
- new_props: float32 [64, 8, 5, 4096], P('cell', 'sec')
The draws below stay inside these ranges and needn't reach their ends.
Inputs may be any that keep to these rules, and one draw needn't show every extreme that they name: `fft_iters`: some cell has exactly 8 FFT iterations and some exactly 2. `rm_iters`: some cell has exactly 3 Newton steps and some exactly 1. move_flag[e, g] equals move_flag[(e + 32) mod 64, g].
All inputs are finite; a program needn't handle non-finite values.
Results may differ from the reference program's by a relative error of at most 0.0003.
Values sent between devices are 32-bit elements; how exact they have to be, the bound alone decides.
No kernel may reach another device: no remote copies, remote signals or barrier semaphores. Data moves between devices by JAX's collectives and lax.ppermute only.
A program may use at most 64 MiB of HBM per device.

```python
import math
import jax
import jax.numpy as jnp
import numpy as np
from jax import lax

GRID = 16
GAUSS = 8
ITMAX = 8
RMAX = 3
EL_DEV = 4
ELEMS = 64
VOX = 4096


def heavy_cells(key):
    groups = ELEMS // EL_DEV
    heavy_mask = jax.random.randint(jax.random.fold_in(key, 17), (groups, GAUSS), 0, 4) == 0
    heavy_mask = heavy_mask.at[0, 0].set(True)
    return jnp.repeat(heavy_mask, EL_DEV, axis=0)


def draw_fft_iters(key, part):
    heavy_mask = heavy_cells(key)
    upper_draw = jax.random.randint(jax.random.fold_in(key, 3), (ELEMS, GAUSS), ITMAX - 1, ITMAX + 1)
    lower_draw = jax.random.randint(jax.random.fold_in(key, 5), (ELEMS, GAUSS), 2, 4)
    counts = jnp.where(heavy_mask, upper_draw, lower_draw)
    counts = counts.at[0, 0].set(ITMAX)
    return counts.at[ELEMS - 1, GAUSS - 1].set(2)


def draw_rm_iters(key, part):
    counts = jax.random.randint(jax.random.fold_in(key, 7), (ELEMS, GAUSS), 1, RMAX + 1)
    counts = counts.at[0, 1].set(RMAX)
    return counts.at[1, 0].set(1)


def draw_move_flag(key, part):
    pair_rows = ELEMS // 2
    first_half = jax.random.randint(jax.random.fold_in(key, 9), (pair_rows, GAUSS), 0, 2)
    first_half = first_half.at[0, 0].set(1).at[0, 1].set(0)
    return jnp.concatenate([first_half, first_half], axis=0)


def block_scale(stream_key, extent, shards, least, largest):
    loudness = 1.0
    for dim, blocks in shards:
        draws = jax.random.uniform(jax.random.fold_in(jax.random.fold_in(stream_key, 6), dim), (blocks,), jnp.float32, least / len(shards), largest / len(shards))
        loudness = loudness * jnp.repeat(jnp.exp(draws), extent[dim] // blocks).reshape((-1,) + (1,) * (len(extent) - 1 - dim))
    return loudness


def gaussian(stream_key, shape, scale, most, split=(), kind=jnp.bfloat16):
    loudness = block_scale(stream_key, shape, split, -0.22, 0.18) if split else 1.0
    entries = jax.random.normal(stream_key, shape, jnp.float32) * scale * loudness
    return jnp.minimum(jnp.maximum(entries, -most), most).astype(kind)


def setup_inputs(seed: int = 0) -> dict:
    key_of = jax.random.split(jax.random.key(seed), 12)
    elem_disp = gaussian(key_of[0], (ELEMS, 24), 0.15, 0.9, ((0, 16),), jnp.float32)
    plastic_strain = gaussian(key_of[1], (ELEMS, GAUSS, 6, VOX), 0.01, 0.06, ((0, 16), (1, 2)), jnp.float32)
    hardening_var = jnp.clip(0.1 * jax.random.uniform(key_of[2], (ELEMS, GAUSS, VOX), jnp.float32) ** block_scale(key_of[2], (ELEMS, GAUSS, VOX), ((0, 16), (1, 2)), -0.2, 0.2), 0.0, 0.1)
    shear_mod = jnp.clip(jnp.exp(math.log(4.0) - 2.0794415 * jax.random.uniform(key_of[3], (ELEMS, GAUSS, VOX), jnp.float32) ** block_scale(key_of[3], (ELEMS, GAUSS, VOX), ((0, 16), (1, 2)), -0.2, 0.2)), 0.5, 4.0)
    bulk_mod = jnp.clip(jnp.exp(math.log(8.0) - 1.6739764 * jax.random.uniform(key_of[4], (ELEMS, GAUSS, VOX), jnp.float32) ** block_scale(key_of[4], (ELEMS, GAUSS, VOX), ((0, 16), (1, 2)), -0.2, 0.2)), 1.5, 8.0)
    yield_stress = jnp.clip(jnp.exp(math.log(0.4) - 1.3862944 * jax.random.uniform(key_of[5], (ELEMS, GAUSS, VOX), jnp.float32) ** block_scale(key_of[5], (ELEMS, GAUSS, VOX), ((0, 16), (1, 2)), -0.2, 0.2)), 0.1, 0.4)
    sat_stress = jnp.clip(jnp.exp(math.log(0.3) - 1.7917595 * jax.random.uniform(key_of[6], (ELEMS, GAUSS, VOX), jnp.float32) ** block_scale(key_of[6], (ELEMS, GAUSS, VOX), ((0, 16), (1, 2)), -0.2, 0.2)), 0.05, 0.3)
    sat_rate = jnp.clip(jnp.exp(math.log(50.0) - 2.3025851 * jax.random.uniform(key_of[7], (ELEMS, GAUSS, VOX), jnp.float32) ** block_scale(key_of[7], (ELEMS, GAUSS, VOX), ((0, 16), (1, 2)), -0.2, 0.2)), 5.0, 50.0)
    fft_iters = draw_fft_iters(jax.random.fold_in(key_of[11], 71), 0)
    rm_iters = draw_rm_iters(jax.random.fold_in(key_of[11], 71), 0)
    move_flag = draw_move_flag(jax.random.fold_in(key_of[11], 71), 0)
    return dict(elem_disp=elem_disp, plastic_strain=plastic_strain, hardening_var=hardening_var, shear_mod=shear_mod, bulk_mod=bulk_mod, yield_stress=yield_stress, sat_stress=sat_stress, sat_rate=sat_rate, fft_iters=fft_iters, rm_iters=rm_iters, move_flag=move_flag)


hardening_slope = 0.05
top_precision = lax.Precision.HIGHEST

def strain_table():
    root = 1.0 / math.sqrt(3.0)
    table = np.zeros((8, 6, 24), np.float32)
    for gauss_pt in range(8):
        point = [((gauss_pt >> axis_bit & 1) * 2 - 1) * root for axis_bit in range(3)]
        for node in range(8):
            signs = [(node >> axis_bit & 1) * 2 - 1 for axis_bit in range(3)]
            grads = []
            for axis_bit in range(3):
                factor = 2.0 * signs[axis_bit] / 8.0
                for other in range(3):
                    if other != axis_bit:
                        factor = factor * (1.0 + signs[other] * point[other])
                grads.append(factor)
            table[gauss_pt, 0, 3 * node + 0] = grads[0]
            table[gauss_pt, 1, 3 * node + 1] = grads[1]
            table[gauss_pt, 2, 3 * node + 2] = grads[2]
            table[gauss_pt, 3, 3 * node + 1] = 0.5 * grads[2]
            table[gauss_pt, 3, 3 * node + 2] = 0.5 * grads[1]
            table[gauss_pt, 4, 3 * node + 0] = 0.5 * grads[2]
            table[gauss_pt, 4, 3 * node + 2] = 0.5 * grads[0]
            table[gauss_pt, 5, 3 * node + 0] = 0.5 * grads[1]
            table[gauss_pt, 5, 3 * node + 1] = 0.5 * grads[0]
    return table

def yield_curve(level, yield_base, sat_level, sat_rate):
    return yield_base + sat_level * (1.0 - jnp.exp(-sat_rate * level)) + hardening_slope * level

def yield_slope(level, sat_level, sat_rate):
    return sat_level * sat_rate * jnp.exp(-sat_rate * level) + hardening_slope

def return_state(strain_field, record, newton_count):
    plastic_old = record[0:6]
    alpha_old = record[6]
    shear_local = record[7]
    bulk_local = record[8]
    yield_base = record[9]
    sat_level = record[10]
    rate_local = record[11]
    normal_vec = jnp.array([1.0, 1.0, 1.0, 0.0, 0.0, 0.0], jnp.float32)[:, None]
    elastic = strain_field - plastic_old
    volume = elastic[0] + elastic[1] + elastic[2]
    trial_dev = 2.0 * shear_local * (elastic - normal_vec * volume / 3.0)
    squared = trial_dev[0] ** 2 + trial_dev[1] ** 2 + trial_dev[2] ** 2 + 2.0 * (trial_dev[3] ** 2 + trial_dev[4] ** 2 + trial_dev[5] ** 2)
    trial_eq = jnp.sqrt(1.5 * squared)
    excess = trial_eq - yield_curve(alpha_old, yield_base, sat_level, rate_local)

    def newton(count_index, increment):
        level = alpha_old + increment
        residual = trial_eq - 3.0 * shear_local * increment - yield_curve(level, yield_base, sat_level, rate_local)
        update = increment + residual / (3.0 * shear_local + yield_slope(level, sat_level, rate_local))
        return jnp.where(count_index < newton_count, update, increment)
    increment = lax.fori_loop(0, RMAX, newton, jnp.zeros_like(trial_eq))
    increment = jnp.where(excess > 0.0, increment, 0.0)
    safe_eq = jnp.maximum(trial_eq, yield_base)
    shrink = 1.0 - 3.0 * shear_local * increment / safe_eq
    stress = bulk_local * volume * normal_vec + shrink * trial_dev
    plastic_new = plastic_old + 1.5 * increment * trial_dev / safe_eq
    alpha_new = alpha_old + increment
    return (stress, plastic_new, alpha_new, (trial_dev, safe_eq, shrink, excess))

def mean_tangent(record, alpha_new, extras):
    trial_dev, safe_eq, shrink, excess = extras
    shear_local = record[7]
    bulk_local = record[8]
    unit_dir = trial_dev / (safe_eq * math.sqrt(2.0 / 3.0))
    slope_new = yield_slope(alpha_new, record[10], record[11])
    correction = jnp.where(excess > 0.0, 3.0 * shear_local / (3.0 * shear_local + slope_new) - (1.0 - shrink), 0.0)
    weighted = 2.0 * shear_local * correction * unit_dir
    outer = jnp.einsum('cv,dv->cd', weighted, unit_dir, precision=top_precision) / unit_dir.shape[1]
    block = jnp.asarray(np.outer([1.0, 1.0, 1.0, 0.0, 0.0, 0.0], [1.0, 1.0, 1.0, 0.0, 0.0, 0.0]).astype(np.float32))
    identity = jnp.eye(6, dtype=jnp.float32)
    weights_vec = jnp.array([1.0, 1.0, 1.0, 2.0, 2.0, 2.0], jnp.float32)
    tangent = jnp.mean(bulk_local) * block + jnp.mean(2.0 * shear_local * shrink) * (identity - block / 3.0) - outer * weights_vec[None, :]
    return tangent.reshape(36)

def green_terms(spec, wave_x, wave_y, wave_z, inv_sq, mu_ref, coupling):
    comp_a = spec[0] * wave_x + spec[5] * wave_y + spec[4] * wave_z
    comp_b = spec[5] * wave_x + spec[1] * wave_y + spec[3] * wave_z
    comp_c = spec[4] * wave_x + spec[3] * wave_y + spec[2] * wave_z
    project = (wave_x * comp_a + wave_y * comp_b + wave_z * comp_c) * inv_sq
    scale = inv_sq / mu_ref
    vec_a = (comp_a - coupling * project * wave_x) * scale
    vec_b = (comp_b - coupling * project * wave_y) * scale
    vec_c = (comp_c - coupling * project * wave_z) * scale
    return jnp.stack([wave_x * vec_a, wave_y * vec_b, wave_z * vec_c, 0.5 * (wave_y * vec_c + wave_z * vec_b), 0.5 * (wave_x * vec_c + wave_z * vec_a), 0.5 * (wave_x * vec_b + wave_y * vec_a)])

def green_apply(stress, mu_ref, coupling):
    waves = jnp.sin(2.0 * jnp.pi * jnp.arange(GRID).astype(jnp.float32) / GRID)
    wave_x = waves[:, None, None]
    wave_y = waves[None, :, None]
    wave_z = waves[None, None, :]
    squared = wave_x ** 2 + wave_y ** 2 + wave_z ** 2
    inv_sq = jnp.where(squared > 0.01, 1.0 / jnp.maximum(squared, 0.01), 0.0)
    spectrum = jnp.fft.fftn(stress.reshape(6, GRID, GRID, GRID), axes=(1, 2, 3))
    mapped = green_terms(spectrum, wave_x, wave_y, wave_z, inv_sq, mu_ref, coupling)
    return jnp.real(jnp.fft.ifftn(mapped, axes=(1, 2, 3))).reshape(6, VOX)

def solve_cell(inputs):
    record, strain_vec, fft_count, newton_count = inputs
    mu_ref = 0.5 * (jnp.max(record[7]) + jnp.min(record[7]))
    bulk_ref = 0.5 * (jnp.max(record[8]) + jnp.min(record[8]))
    lame_ref = bulk_ref - 2.0 * mu_ref / 3.0
    coupling = (lame_ref + mu_ref) / (lame_ref + 2.0 * mu_ref)
    field = strain_vec[:, None] * jnp.ones((1, VOX), jnp.float32)

    def sweep(sweep_index, current):
        stress = return_state(current, record, newton_count)[0]
        return jnp.where(sweep_index < fft_count, current - green_apply(stress, mu_ref, coupling), current)
    field = lax.fori_loop(0, ITMAX, sweep, field)
    stress, plastic_new, alpha_new, extras = return_state(field, record, newton_count)
    tangent = mean_tangent(record, alpha_new, extras)
    new_record = jnp.concatenate([plastic_new, alpha_new[None], record[7:]], axis=0)
    return (new_record, lax.optimization_barrier(jnp.mean(stress, axis=1)), tangent)

def reference(elem_disp, plastic_strain, hardening_var, shear_mod, bulk_mod, yield_stress, sat_stress, sat_rate, fft_iters, rm_iters, move_flag):
    table = jnp.asarray(strain_table())
    strain = jnp.einsum('gcn,en->egc', table, elem_disp, precision=top_precision)
    props = jnp.stack([shear_mod, bulk_mod, yield_stress, sat_stress, sat_rate], axis=2)
    record = jnp.concatenate([plastic_strain, hardening_var[:, :, None, :], props], axis=2)
    total = ELEMS * GAUSS
    new_rec, stress, tangent = lax.map(solve_cell, (record.reshape(total, 12, VOX), strain.reshape(total, 6), fft_iters.reshape(total), rm_iters.reshape(total)))
    new_rec = new_rec.reshape(ELEMS, GAUSS, 12, VOX)
    stress = stress.reshape(ELEMS, GAUSS, 6)
    tangent = tangent.reshape(ELEMS, GAUSS, 6, 6)
    rolled = jnp.roll(new_rec, ELEMS // 2, axis=0)
    moved = jnp.where(move_flag[:, :, None, None] > 0, rolled, new_rec)
    weights_vec = jnp.array([1.0, 1.0, 1.0, 2.0, 2.0, 2.0], jnp.float32)
    force = jnp.einsum('egc,gcn->en', stress * weights_vec, table, precision=top_precision) / GAUSS
    scaled = tangent * weights_vec[None, None, :, None]
    stiff = jnp.einsum('gcn,egcd,gdm->enm', table, scaled, table, precision=top_precision).reshape(ELEMS, 576) / GAUSS
    return (force, stiff, stress, moved[:, :, 0:7], moved[:, :, 7:12])
```

```python
import functools
import math

import jax
import jax.numpy as jnp
import numpy as np
from jax import lax
from jax.experimental import pallas as pl
from jax.experimental.pallas import tpu as pltpu
from jax.sharding import PartitionSpec as P

GRID = 16
PLANE = GRID * GRID
LANES = 128
BATCH = 8
GAUSS = 8
SLOPE = 0.05
top_precision = lax.Precision.HIGHEST
SUMS = 29


def strain_table():
    root = 1.0 / math.sqrt(3.0)
    table = np.zeros((8, 6, 24), np.float32)
    for gauss_pt in range(8):
        point = [((gauss_pt >> axis_bit & 1) * 2 - 1) * root for axis_bit in range(3)]
        for node in range(8):
            signs = [(node >> axis_bit & 1) * 2 - 1 for axis_bit in range(3)]
            grads = []
            for axis_bit in range(3):
                factor = 2.0 * signs[axis_bit] / 8.0
                for other in range(3):
                    if other != axis_bit:
                        factor = factor * (1.0 + signs[other] * point[other])
                grads.append(factor)
            table[gauss_pt, 0, 3 * node + 0] = grads[0]
            table[gauss_pt, 1, 3 * node + 1] = grads[1]
            table[gauss_pt, 2, 3 * node + 2] = grads[2]
            table[gauss_pt, 3, 3 * node + 1] = 0.5 * grads[2]
            table[gauss_pt, 3, 3 * node + 2] = 0.5 * grads[1]
            table[gauss_pt, 4, 3 * node + 0] = 0.5 * grads[2]
            table[gauss_pt, 4, 3 * node + 2] = 0.5 * grads[0]
            table[gauss_pt, 5, 3 * node + 0] = 0.5 * grads[1]
            table[gauss_pt, 5, 3 * node + 1] = 0.5 * grads[0]
    return table


def cas_tables():
    index = np.arange(GRID)
    angle = 2.0 * np.pi * (np.outer(index, index) % GRID) / GRID
    plus = np.cos(angle) + np.sin(angle)
    minus = np.cos(angle) - np.sin(angle)
    full = np.stack(
        [np.kron(plus, plus), -np.kron(minus, minus), -np.kron(plus, minus), -np.kron(minus, plus)]
    ).astype(np.float32)
    high = full.astype(jnp.bfloat16)
    low = (full - high.astype(np.float32)).astype(jnp.bfloat16)
    waves = np.sin(2.0 * np.pi * index / GRID)
    wave_y = np.repeat(waves, GRID)
    wave_z = np.tile(waves, GRID)
    squared = waves[:, None] ** 2 + wave_y[None, :] ** 2 + wave_z[None, :] ** 2
    inv_sq = np.where(squared > 0.01, 1.0 / np.maximum(squared, 0.01), 0.0)
    table = np.concatenate([inv_sq, wave_y[None], wave_z[None], np.zeros((6, PLANE))], axis=0)
    return high, low, table.astype(np.float32), [float(w) for w in waves]


def hartley(values):
    count = len(values)
    if count == 1:
        return list(values)
    half = count // 2
    even = hartley(values[0::2])
    odd = hartley(values[1::2])
    low, high = [], []
    for k in range(half):
        other = odd[(-k) % half]
        if k == 0:
            term = odd[0]
        elif 4 * k == count:
            term = other
        elif 8 * k == count:
            term = (odd[k] + other) * math.sqrt(0.5)
        elif 8 * k == 3 * count:
            term = (other - odd[k]) * math.sqrt(0.5)
        else:
            turn = 2.0 * math.pi * k / count
            term = odd[k] * math.cos(turn) + other * math.sin(turn)
        low.append(even[k] + term)
        high.append(even[k] - term)
    return low + high


def pack_kernel(
    elems, points, first, flag, shear, bulk, base, sat, rate, hard, order, head, tail, alpha
):
    total = elems * points

    def place(wanted, start):
        def step(cell, at):
            hit = (flag[cell // points, cell % points] > 0) == wanted

            @pl.when(hit)
            def _():
                order[at] = cell

            return at + hit.astype(jnp.int32)

        return lax.fori_loop(0, total, step, start)

    moving = place(True, jnp.int32(0))
    place(False, moving)
    order[total] = moving

    def copy_row(source, cell, target, slot, row):
        for x in range(GRID):
            target[slot, row * GRID + x : row * GRID + x + 1, :] = source[
                cell // points, pl.ds(cell % points, 1), x * PLANE : (x + 1) * PLANE
            ]

    def fill(target, begin, count):
        def step(slot, carry):
            cell = order[begin + slot]
            for row, source in enumerate((shear, bulk, base, sat, rate)):
                copy_row(source, cell, target, slot, row)
            copy_row(hard, cell, alpha, begin + slot, 0)
            return carry

        lax.fori_loop(0, count, step, 0)

    fill(head, 0, first)
    fill(tail, first, total - first)


def solve_kernel(
    elems,
    points,
    begin,
    waves,
    order,
    fft_iters,
    rm_iters,
    strain,
    plastic,
    props,
    alpha,
    high,
    low,
    table,
    state,
    sums,
    rec,
    field,
    work,
    spec,
    part_hi,
    part_lo,
    acc,
):
    total = elems * points
    block = GRID * BATCH
    row_of = lax.broadcasted_iota(jnp.int32, (BATCH, LANES), 0)

    cells = [order[min(begin + slot, total - 1)] for slot in range(BATCH)]

    for slot, cell in enumerate(cells):
        e_at, g_at = cell // points, cell % points
        slot_in = min(begin + slot, total - 1)
        own = min(slot, props.shape[0] - 1)
        for x in range(GRID):
            for half in range(2):
                lane = half * LANES
                rec[half, pl.ds(x * BATCH + slot, 6, stride=block), :] = plastic[
                    e_at, g_at, :, x * PLANE + lane : x * PLANE + lane + LANES
                ]
        for half in range(2):
            lane = half * LANES
            for part in range(2):
                rec[half, pl.ds(6 * block + part * 64 + slot, 8, stride=BATCH), :] = alpha[
                    slot_in, part * 8 : part * 8 + 8, lane : lane + LANES
                ]
                for row in range(5):
                    at = row * GRID + part * 8
                    rec[half, pl.ds((7 + row) * block + part * 64 + slot, 8, stride=BATCH), :] = (
                        props[own, at : at + 8, lane : lane + LANES]
                    )

    def per_cell(pick, dtype):
        out = jnp.zeros((BATCH, LANES), dtype)
        for slot in range(BATCH):
            out = jnp.where(row_of == slot, pick(slot), out)
        return out

    fft_count = per_cell(lambda s: fft_iters[cells[s] // points, cells[s] % points], jnp.int32)
    rm_count = per_cell(lambda s: rm_iters[cells[s] // points, cells[s] % points], jnp.int32)
    most = functools.reduce(
        jnp.maximum, [fft_iters[c // points, c % points] for c in cells]
    )

    def extremes(row):
        top = bottom = None
        for half in range(2):
            for x in range(GRID):
                value = rec[half, row * block + x * BATCH : row * block + (x + 1) * BATCH, :]
                top = value if top is None else jnp.maximum(top, value)
                bottom = value if bottom is None else jnp.minimum(bottom, value)
        return 0.5 * (
            jnp.max(top, axis=1, keepdims=True) + jnp.min(bottom, axis=1, keepdims=True)
        )

    mu_ref = extremes(7)
    bulk_ref = extremes(8)
    lame_ref = bulk_ref - 2.0 * mu_ref / 3.0
    coupling = jnp.broadcast_to((lame_ref + mu_ref) / (lame_ref + 2.0 * mu_ref), (BATCH, LANES))
    inv_mu = jnp.broadcast_to(1.0 / (mu_ref * (GRID * PLANE)), (BATCH, LANES))

    for comp in range(6):
        value = per_cell(lambda s: strain[cells[s] // points, cells[s] % points, comp], jnp.float32)
        value = jnp.concatenate([value] * 2, axis=0)

        def start(pair, carry):
            for half in range(2):
                field[half, pl.ds(comp * block + pair * 16, 16), :] = value
            return carry

        lax.fori_loop(0, GRID // 2, start, 0)

    def prepare(pair, carry):
        for half in range(2):
            load = lambda row: rec[half, pl.ds(row * block + pair * 16, 16), :]
            level, mu, sat, rate = load(6), load(7), load(10), load(11)
            decay = jnp.exp(-rate * level)
            rec[half, pl.ds(12 * block + pair * 16, 16), :] = (
                load(9) + sat * (1.0 - decay) + SLOPE * level
            )
            rest = sat * decay
            rec[half, pl.ds(13 * block + pair * 16, 16), :] = rest
            rec[half, pl.ds(14 * block + pair * 16, 16), :] = 1.0 / (
                3.0 * mu + rest * rate + SLOPE
            )
        return carry

    lax.fori_loop(0, GRID // 2, prepare, 0)

    rm_pair = jnp.concatenate([rm_count] * 2, axis=0)
    second, third = rm_pair > 1, rm_pair > 2

    def newton(over, inc, mu3, rest, rate):
        decay = jnp.exp(-rate * inc)
        num = over - mu3 * inc - rest * (1.0 - decay)
        return inc + num / (mu3 + rest * rate * decay)

    def trial(half, pair):
        load = lambda row: rec[half, pl.ds(row * block + pair * 16, 16), :]
        elastic = [
            field[half, pl.ds(comp * block + pair * 16, 16), :] - load(comp) for comp in range(6)
        ]
        volume = elastic[0] + elastic[1] + elastic[2]
        mu = load(7)
        mu2 = 2.0 * mu
        mean = volume * (1.0 / 3.0)
        dev = [mu2 * (part - mean) for part in elastic[:3]] + [mu2 * part for part in elastic[3:]]
        squared = 1.5 * (dev[0] * dev[0] + dev[1] * dev[1] + dev[2] * dev[2]) + 3.0 * (
            dev[3] * dev[3] + dev[4] * dev[4] + dev[5] * dev[5]
        )
        return load, volume, mu, dev, squared

    def increments(load, mu, over):
        mu3 = 3.0 * mu + SLOPE
        rest, rate = load(13), load(11)
        inc = over * load(14)
        inc = jnp.where(second, newton(over, inc, mu3, rest, rate), inc)
        return jnp.where(third, newton(over, inc, mu3, rest, rate), inc)

    def stress_step(pair, carry):
        for half in range(2):
            load, volume, mu, dev, squared = trial(half, pair)
            base = load(9)
            capped = jnp.maximum(squared, base * base)
            inv_eq = lax.rsqrt(capped)
            over = jnp.maximum(capped * inv_eq - load(12), 0.0)
            inc = increments(load, mu, over)
            shrink = 1.0 - 3.0 * mu * inc * inv_eq
            pressure = load(8) * volume
            for comp in range(6):
                value = shrink * dev[comp]
                if comp < 3:
                    value = value + pressure
                upper = value.astype(jnp.bfloat16)
                at = pl.ds(comp * block + pair * 16, 16)
                lanes = slice(half * LANES, (half + 1) * LANES)
                part_hi[at, lanes] = upper
                part_lo[at, lanes] = (value - upper.astype(jnp.float32)).astype(jnp.bfloat16)
        return carry

    def plane_product(store):
        for which, (from_row, rows) in enumerate(
            ((0, 3 * block), (3 * block, block), (4 * block, block), (5 * block, block))
        ):
            for at in range(from_row, from_row + rows, block):
                left_hi = part_hi[at : at + block, :]
                left_lo = part_lo[at : at + block, :]
                dot = functools.partial(jnp.dot, preferred_element_type=jnp.float32)
                store(
                    at,
                    dot(left_hi, high[which])
                    + (dot(left_lo, high[which]) + dot(left_hi, low[which])),
                )

    def store_spec(at, value):
        for half in range(2):
            work[half, at : at + block, :] = value[:, half * LANES : (half + 1) * LANES]

    def update_field(at, value):
        for half in range(2):
            field[half, at : at + block, :] = (
                field[half, at : at + block, :] - value[:, half * LANES : (half + 1) * LANES]
            )

    def flip(comp, k):
        return (-k) % GRID if comp in (4, 5) else k

    def sweep(index, carry):
        lax.fori_loop(0, GRID // 2, stress_step, 0)
        plane_product(store_spec)
        scale_cell = jnp.where(index < fft_count, inv_mu, 0.0)

        def spectral(half, inner):
            for comp in range(6):
                lines = hartley(
                    [
                        work[half, comp * block + x * BATCH : comp * block + (x + 1) * BATCH, :]
                        for x in range(GRID)
                    ]
                )
                for k in range(GRID):
                    at = comp * block + flip(comp, k) * BATCH
                    spec[half, at : at + BATCH, :] = lines[k]
            wave_y = jnp.broadcast_to(table[half, GRID : GRID + 1, :], (BATCH, LANES))
            wave_z = jnp.broadcast_to(table[half, GRID + 1 : GRID + 2, :], (BATCH, LANES))
            for k in range(GRID):
                wave_x = waves[k]
                inv_sq = jnp.broadcast_to(table[half, k : k + 1, :], (BATCH, LANES))
                s = [
                    spec[half, comp * block + k * BATCH : comp * block + (k + 1) * BATCH, :]
                    for comp in range(6)
                ]
                comp_a = s[0] * wave_x + s[5] * wave_y + s[4] * wave_z
                comp_b = s[5] * wave_x + s[1] * wave_y + s[3] * wave_z
                comp_c = s[4] * wave_x + s[3] * wave_y + s[2] * wave_z
                along = (wave_x * comp_a + wave_y * comp_b + wave_z * comp_c) * (
                    inv_sq * coupling
                )
                scale = inv_sq * scale_cell
                vec_a = (comp_a - along * wave_x) * scale
                vec_b = (comp_b - along * wave_y) * scale
                vec_c = (comp_c - along * wave_z) * scale
                mapped = (
                    wave_x * vec_a,
                    wave_y * vec_b,
                    wave_z * vec_c,
                    0.5 * (wave_y * vec_c + wave_z * vec_b),
                    0.5 * (wave_x * vec_c + wave_z * vec_a),
                    0.5 * (wave_x * vec_b + wave_y * vec_a),
                )
                for comp in range(6):
                    at = comp * block + flip(comp, k) * BATCH
                    work[half, at : at + BATCH, :] = mapped[comp]
            return inner

        for half in range(2):
            spectral(half, 0)
            for comp in range(6):
                lines = hartley(
                    [
                        work[half, comp * block + x * BATCH : comp * block + (x + 1) * BATCH, :]
                        for x in range(GRID)
                    ]
                )
                for pair in range(GRID // 2):
                    value = jnp.concatenate([lines[2 * pair], lines[2 * pair + 1]], axis=0)
                    upper = value.astype(jnp.bfloat16)
                    at = comp * block + pair * 16
                    lanes = slice(half * LANES, (half + 1) * LANES)
                    part_hi[at : at + 16, lanes] = upper
                    part_lo[at : at + 16, lanes] = (value - upper.astype(jnp.float32)).astype(
                        jnp.bfloat16
                    )
        plane_product(update_field)
        return carry

    lax.fori_loop(0, most, sweep, 0)

    acc[...] = jnp.zeros_like(acc)

    def finish(pair, carry):
        for half in range(2):
            load, volume, mu, dev, squared = trial(half, pair)
            base = load(9)
            trial_eq = jnp.sqrt(squared)
            excess = trial_eq - load(12)
            over = jnp.maximum(excess, 0.0)
            inc = increments(load, mu, over)
            inv_eq = 1.0 / jnp.maximum(trial_eq, base)
            lost = 3.0 * mu * inc * inv_eq
            shrink = 1.0 - lost
            pressure = load(8) * volume
            grow = 1.5 * inc * inv_eq
            for comp in range(6):
                work[half, pl.ds(comp * block + pair * 16, 16), :] = load(comp) + grow * dev[comp]
            spec[half, pl.ds(pair * 16, 16), :] = load(6) + inc
            rate = load(11)
            slope = load(13) * rate * jnp.exp(-rate * inc) + SLOPE
            corr = jnp.where(excess > 0.0, 3.0 * mu / (3.0 * mu + slope) - lost, 0.0)
            weight = 3.0 * mu * corr * (inv_eq * inv_eq)
            terms = [shrink * part for part in dev]
            terms = [term + pressure for term in terms[:3]] + terms[3:]
            terms.append(load(8))
            terms.append(2.0 * mu * shrink)
            for c in range(6):
                scaled = weight * dev[c]
                for d in range(c, 6):
                    terms.append(scaled * dev[d])
            for at, term in enumerate(terms):
                acc[at] = acc[at] + (term[:BATCH] + term[BATCH:])
        return carry

    lax.fori_loop(0, GRID // 2, finish, 0)

    lane_of = lax.broadcasted_iota(jnp.int32, (BATCH, LANES), 1)
    out = jnp.zeros((BATCH, LANES), jnp.float32)
    for at in range(SUMS):
        out = jnp.where(lane_of == at, jnp.sum(acc[at], axis=1, keepdims=True), out)
    sums[...] = out * (1.0 / (GRID * PLANE))

    for slot in range(BATCH):
        for half in range(2):
            lanes = slice(half * LANES, (half + 1) * LANES)
            for row in range(7):
                source, from_row = (work, row) if row < 6 else (spec, 0)
                for part in range(2):
                    at = row * GRID + part * 8
                    state[slot, at : at + 8, lanes] = source[
                        half, pl.ds(from_row * block + part * 64 + slot, 8, stride=BATCH), :
                    ]


def spread_rows(source, slot, rows, target):
    for x in range(GRID):
        for half in range(2):
            lane = x * PLANE + half * LANES
            target[slot, :, lane : lane + LANES] = source[
                slot, half, pl.ds(x, rows, stride=GRID), :
            ]


def merge_kernel(
    total, points, first, local_cells, aliased, order, p_head, p_tail, s_head, s_tail, *refs
):
    if aliased:
        refs = refs[2:]
    new_state, new_props, p_in, s_in, p_out, s_out, in_sem, out_sem = refs
    moving = order[total]
    begin, end = (moving, total) if local_cells else (0, moving)

    def arrivals(slot, act):
        def both(source_p, source_s, at):
            for half in range(2):
                lanes = pl.ds(half * LANES, LANES)
                act(
                    pltpu.make_async_copy(
                        source_p.at[at, :, lanes], p_in.at[slot, half], in_sem.at[slot]
                    )
                )
                act(
                    pltpu.make_async_copy(
                        source_s.at[at, :, lanes], s_in.at[slot, half], in_sem.at[slot]
                    )
                )

        @pl.when(slot < first)
        def _():
            both(p_head, s_head, slot)

        @pl.when(slot >= first)
        def _():
            both(p_tail, s_tail, slot - first)

    def departures(slot, act):
        cell = order[slot]
        e_at, g_at = cell // points, cell % points
        act(pltpu.make_async_copy(p_out.at[slot], new_props.at[e_at, g_at], out_sem.at[slot]))
        act(pltpu.make_async_copy(s_out.at[slot], new_state.at[e_at, g_at], out_sem.at[slot]))

    @pl.loop(begin, end)
    def _(slot):
        arrivals(slot, lambda copy: copy.start())

    @pl.loop(begin, end)
    def _(slot):
        arrivals(slot, lambda copy: copy.wait())
        spread_rows(p_in, slot, 5, p_out)
        spread_rows(s_in, slot, 7, s_out)
        departures(slot, lambda copy: copy.start())

    @pl.loop(begin, end)
    def _(slot):
        departures(slot, lambda copy: copy.wait())


def element_terms(table_part, sums, points):
    elems = sums.shape[0] // points
    weights = np.array([1.0, 1.0, 1.0, 2.0, 2.0, 2.0], np.float32)
    stress = sums[:, 0:6]
    block = np.outer([1.0, 1.0, 1.0, 0.0, 0.0, 0.0], [1.0, 1.0, 1.0, 0.0, 0.0, 0.0])
    spread = np.zeros((23, 36), np.float32)
    spread[0] = block.reshape(36)
    spread[1] = (np.eye(6) - block / 3.0).reshape(36)
    at = 2
    for c in range(6):
        for d in range(c, 6):
            spread[at, 6 * c + d] = -weights[d]
            spread[at, 6 * d + c] = -weights[c]
            at += 1
    tangent = jnp.dot(sums[:, 6:SUMS], spread, precision=top_precision)
    stress_part = stress.reshape(elems, points, 6)
    force = (
        jnp.einsum("egc,gcn->en", stress_part * weights, table_part, precision=top_precision)
        / GAUSS
    )
    scaled = tangent.reshape(elems, points, 6, 6) * weights[None, None, :, None]
    stiff = (
        jnp.einsum(
            "gcn,egcd,gdm->enm", table_part, scaled, table_part, precision=top_precision
        ).reshape(elems, 576)
        / GAUSS
    )
    return stress_part, jnp.concatenate([force, stiff], axis=1)


VMEM = pl.BlockSpec(memory_space=pltpu.VMEM)
SMEM = pl.BlockSpec(memory_space=pltpu.SMEM)
ANY = pl.BlockSpec(memory_space=pl.ANY)
GRANT = 60 * 2**20


def shape(*dims, dtype=jnp.float32):
    return jax.ShapeDtypeStruct(dims, dtype)


def local(
    elem_disp,
    plastic_strain,
    hardening_var,
    shear_mod,
    bulk_mod,
    yield_stress,
    sat_stress,
    sat_rate,
    fft_iters,
    rm_iters,
    move_flag,
):
    elems, points = plastic_strain.shape[:2]
    voxels = plastic_strain.shape[3]
    total = elems * points
    first = min(BATCH, total)
    rest = total - first
    tail_slots = max(rest, 1)
    devices = lax.axis_size("cell")
    route = [((i - devices // 2) % devices, i) for i in range(devices)]

    params = pltpu.CompilerParams(vmem_limit_bytes=GRANT)
    order, p_head, p_tail, alpha = pl.pallas_call(
        functools.partial(pack_kernel, elems, points, first),
        out_shape=(
            shape(total + 1, dtype=jnp.int32),
            shape(first, 5 * GRID, PLANE),
            shape(tail_slots, 5 * GRID, PLANE),
            shape(total, GRID, PLANE),
        ),
        in_specs=[SMEM] + [VMEM] * 6,
        out_specs=(SMEM, VMEM, VMEM, VMEM),
        compiler_params=params,
        name="pack",
    )(move_flag, shear_mod, bulk_mod, yield_stress, sat_stress, sat_rate, hardening_var)

    got_p_head = lax.ppermute(p_head, "cell", route)

    full_table = jnp.asarray(strain_table())
    table_part = lax.dynamic_slice_in_dim(full_table, lax.axis_index("sec") * points, points, 0)
    strain = jnp.einsum("gcn,en->egc", table_part, elem_disp, precision=top_precision)

    high, low, table, waves = cas_tables()
    table = table.reshape(24, 2, LANES).transpose(1, 0, 2)
    block = GRID * BATCH

    def solve(begin, props):
        return pl.pallas_call(
            functools.partial(solve_kernel, elems, points, begin, waves),
            out_shape=(shape(BATCH, 7 * GRID, PLANE), shape(BATCH, LANES)),
            in_specs=[SMEM] * 4 + [VMEM] * 6,
            out_specs=(VMEM, VMEM),
            scratch_shapes=[
                pltpu.VMEM((2, 15 * block, LANES), jnp.float32),
                pltpu.VMEM((2, 6 * block, LANES), jnp.float32),
                pltpu.VMEM((2, 6 * block, LANES), jnp.float32),
                pltpu.VMEM((2, 6 * block, LANES), jnp.float32),
                pltpu.VMEM((6 * block, PLANE), jnp.bfloat16),
                pltpu.VMEM((6 * block, PLANE), jnp.bfloat16),
                pltpu.VMEM((SUMS, BATCH, LANES), jnp.float32),
            ],
            compiler_params=params,
            cost_estimate=pl.CostEstimate(
                flops=20 * 10**9, bytes_accessed=8 * 10**6, transcendentals=0
            ),
            name="solve",
        )(order, fft_iters, rm_iters, strain, plastic_strain, props, alpha, high, low, table)

    s_head, sums = solve(0, p_head)
    got_s_head = lax.ppermute(s_head[:first], "cell", route)
    if rest:
        s_tail, more = solve(first, p_tail)
        sums = jnp.concatenate([sums, more], axis=0)
    else:
        s_tail = jnp.zeros((1, 7 * GRID, PLANE), jnp.float32)

    def merge(local_cells, parts, outs=()):
        return pl.pallas_call(
            functools.partial(merge_kernel, total, points, first, local_cells, bool(outs)),
            out_shape=(shape(elems, points, 7, voxels), shape(elems, points, 5, voxels)),
            in_specs=[SMEM] + [ANY] * (4 + len(outs)),
            out_specs=(ANY, ANY),
            scratch_shapes=[
                pltpu.VMEM((total, 2, 5 * GRID, LANES), jnp.float32),
                pltpu.VMEM((total, 2, 7 * GRID, LANES), jnp.float32),
                pltpu.VMEM((total, 5, voxels), jnp.float32),
                pltpu.VMEM((total, 7, voxels), jnp.float32),
                pltpu.SemaphoreType.DMA((total,)),
                pltpu.SemaphoreType.DMA((total,)),
            ],
            input_output_aliases={5: 0, 6: 1} if outs else {},
            compiler_params=params,
            name="merge_own" if local_cells else "merge_moved",
        )(order, *parts, *outs)

    outs = merge(True, (p_head, p_tail, s_head, s_tail))

    slots = order[:total]
    place = (slots[None, :] == jnp.arange(total)[:, None]).astype(jnp.float32)
    sums = jnp.dot(place, sums[:total], precision=top_precision)
    stress, share = element_terms(table_part, sums, points)
    sections = lax.axis_size("sec")
    whole = share
    for step in range(1, sections):
        ring = [((i - step) % sections, i) for i in range(sections)]
        whole = whole + lax.ppermute(share, "sec", ring)

    def branch(count):
        def run(props, state):
            if count == 0:
                return jnp.zeros_like(props), jnp.zeros_like(state)
            pad = ((0, tail_slots - count), (0, 0), (0, 0))
            return (
                jnp.pad(lax.ppermute(props[:count], "cell", route), pad),
                jnp.pad(lax.ppermute(state[:count], "cell", route), pad),
            )

        return run

    if rest:
        extra = jnp.clip(jnp.sum((move_flag > 0).astype(jnp.int32)) - first, 0, rest)
        got_p_tail, got_s_tail = lax.switch(
            extra, [branch(c) for c in range(rest + 1)], p_tail, s_tail
        )
    else:
        got_p_tail, got_s_tail = p_tail, s_tail

    new_state, new_props = merge(False, (got_p_head, got_p_tail, got_s_head, got_s_tail), outs)
    return whole[:, :24], whole[:, 24:], stress, new_state, new_props


def solution(mesh):
    in_specs = (
        P("cell", None),
        P("cell", "sec", None, None),
        P("cell", "sec", None),
        P("cell", "sec", None),
        P("cell", "sec", None),
        P("cell", "sec", None),
        P("cell", "sec", None),
        P("cell", "sec", None),
        P("cell", "sec"),
        P("cell", "sec"),
        P("cell", "sec"),
    )
    out_specs = (
        P("cell", None),
        P("cell", None),
        P("cell", "sec", None),
        P("cell", "sec", None, None),
        P("cell", "sec", None, None),
    )
    return jax.shard_map(local, mesh=mesh, in_specs=in_specs, out_specs=out_specs, check_vma=False)
```

```python
import functools
import math

import jax
import jax.numpy as jnp
import numpy as np
from jax import lax
from jax.experimental import pallas as pl
from jax.experimental.pallas import tpu as pltpu
from jax.sharding import PartitionSpec as P


GRID = 16
PLANE = GRID * GRID
LANES = 128
BATCH = 8
GAUSS = 8
SLOPE = 0.05
top_precision = lax.Precision.HIGHEST
SUMS = 29
LINES = GRID * PLANE // LANES
P_ROWS = 5 * LINES
S_ROWS = 7 * LINES
ROWS = P_ROWS + S_ROWS
EARLY = 6


def strain_table():
    root = 1.0 / math.sqrt(3.0)
    table = np.zeros((8, 6, 24), np.float32)
    for gauss_pt in range(8):
        point = [((gauss_pt >> axis_bit & 1) * 2 - 1) * root for axis_bit in range(3)]
        for node in range(8):
            signs = [(node >> axis_bit & 1) * 2 - 1 for axis_bit in range(3)]
            grads = []
            for axis_bit in range(3):
                factor = 2.0 * signs[axis_bit] / 8.0
                for other in range(3):
                    if other != axis_bit:
                        factor = factor * (1.0 + signs[other] * point[other])
                grads.append(factor)
            table[gauss_pt, 0, 3 * node + 0] = grads[0]
            table[gauss_pt, 1, 3 * node + 1] = grads[1]
            table[gauss_pt, 2, 3 * node + 2] = grads[2]
            table[gauss_pt, 3, 3 * node + 1] = 0.5 * grads[2]
            table[gauss_pt, 3, 3 * node + 2] = 0.5 * grads[1]
            table[gauss_pt, 4, 3 * node + 0] = 0.5 * grads[2]
            table[gauss_pt, 4, 3 * node + 2] = 0.5 * grads[0]
            table[gauss_pt, 5, 3 * node + 0] = 0.5 * grads[1]
            table[gauss_pt, 5, 3 * node + 1] = 0.5 * grads[0]
    return table


def cas_tables():
    index = np.arange(GRID)
    angle = 2.0 * np.pi * (np.outer(index, index) % GRID) / GRID
    plus = np.cos(angle) + np.sin(angle)
    minus = np.cos(angle) - np.sin(angle)
    full = np.stack(
        [np.kron(plus, plus), -np.kron(minus, minus), -np.kron(plus, minus), -np.kron(minus, plus)]
    ).astype(np.float32)
    high = full.astype(jnp.bfloat16)
    low = (full - high.astype(np.float32)).astype(jnp.bfloat16)
    waves = np.sin(2.0 * np.pi * index / GRID)
    wave_y = np.repeat(waves, GRID)
    wave_z = np.tile(waves, GRID)
    squared = waves[:, None] ** 2 + wave_y[None, :] ** 2 + wave_z[None, :] ** 2
    inv_sq = np.where(squared > 0.01, 1.0 / np.maximum(squared, 0.01), 0.0)
    table = np.concatenate([inv_sq, wave_y[None], wave_z[None], np.zeros((6, PLANE))], axis=0)
    return high, low, table.astype(np.float32), [float(w) for w in waves]


def hartley(values):
    count = len(values)
    if count == 1:
        return list(values)
    half = count // 2
    even = hartley(values[0::2])
    odd = hartley(values[1::2])
    low, high = [], []
    for k in range(half):
        other = odd[(-k) % half]
        if k == 0:
            term = odd[0]
        elif 4 * k == count:
            term = other
        elif 8 * k == count:
            term = (odd[k] + other) * math.sqrt(0.5)
        elif 8 * k == 3 * count:
            term = (other - odd[k]) * math.sqrt(0.5)
        else:
            turn = 2.0 * math.pi * k / count
            term = odd[k] * math.cos(turn) + other * math.sin(turn)
        low.append(even[k] + term)
        high.append(even[k] - term)
    return low + high


def pack_kernel(elems, points, first, flag, *refs):
    *sources, order, head = refs
    total = elems * points

    def place(wanted, start):
        def step(cell, at):
            hit = (flag[cell // points, cell % points] > 0) == wanted

            @pl.when(hit)
            def _():
                order[at] = cell
                order[total + 1 + cell] = at

            return at + hit.astype(jnp.int32)

        return lax.fori_loop(0, total, step, start)

    moving = place(True, jnp.int32(0))
    place(False, moving)
    order[total] = moving

    for slot in range(first):
        cell = order[slot]
        at = (cell // points) * (LINES * points) + cell % points
        for row, source in enumerate(sources):
            for part in range(0, LINES, 8):
                head[slot, row * LINES + part : row * LINES + part + 8, :] = source[
                    pl.ds(at + part * points, 8, stride=points), :
                ]


def solve_kernel(
    elems,
    points,
    begin,
    first,
    waves,
    order,
    fft_iters,
    rm_iters,
    disp,
    bmat,
    plastic,
    hard,
    shear,
    bulk,
    base,
    sat,
    rate,
    high,
    low,
    table,
    other,
    after,
    sums,
    rec,
    field,
    work,
    spec,
    part_hi,
    part_lo,
    acc,
):
    total = elems * points
    block = GRID * BATCH
    row_of = lax.broadcasted_iota(jnp.int32, (BATCH, LANES), 0)

    cells = [order[min(begin + slot, total - 1)] for slot in range(BATCH)]

    section = lax.axis_index("sec")

    def fill(slot, carry):
        cell = order[jnp.minimum(begin + slot, total - 1)]
        e_at, g_at = cell // points, cell % points
        for half in range(2):
            for part in range(2):
                near = (part * 16 + half) * points + g_at
                here = part * 64 + slot
                for comp in range(6):
                    at = (e_at * 6 + comp) * (LINES * points) + near
                    rec[half, pl.ds(comp * block + here, 8, stride=BATCH), :] = plastic[
                        pl.ds(at, 8, stride=2 * points), :
                    ]
                for row, source in enumerate((hard, shear, bulk, base, sat, rate)):
                    at = e_at * (LINES * points) + near
                    rec[half, pl.ds((6 + row) * block + here, 8, stride=BATCH), :] = source[
                        pl.ds(at, 8, stride=2 * points), :
                    ]
        value = jnp.sum(bmat[section * points + g_at] * disp[e_at], axis=1, keepdims=True)
        acc[pl.ds(0, 6), pl.ds(slot, 1), :] = jnp.broadcast_to(value, (6, LANES))[:, None, :]
        return carry

    lax.fori_loop(0, BATCH, fill, 0)

    def per_cell(pick, dtype):
        out = jnp.zeros((BATCH, LANES), dtype)
        for slot in range(BATCH):
            out = jnp.where(row_of == slot, pick(slot), out)
        return out

    fft_count = per_cell(lambda s: fft_iters[cells[s] // points, cells[s] % points], jnp.int32)
    rm_count = per_cell(lambda s: rm_iters[cells[s] // points, cells[s] % points], jnp.int32)
    most = functools.reduce(
        jnp.maximum, [fft_iters[c // points, c % points] for c in cells]
    )

    def extremes(row):
        top = bottom = None
        for half in range(2):
            for x in range(GRID):
                value = rec[half, row * block + x * BATCH : row * block + (x + 1) * BATCH, :]
                top = value if top is None else jnp.maximum(top, value)
                bottom = value if bottom is None else jnp.minimum(bottom, value)
        return 0.5 * (
            jnp.max(top, axis=1, keepdims=True) + jnp.min(bottom, axis=1, keepdims=True)
        )

    mu_ref = extremes(7)
    bulk_ref = extremes(8)
    lame_ref = bulk_ref - 2.0 * mu_ref / 3.0
    coupling = jnp.broadcast_to((lame_ref + mu_ref) / (lame_ref + 2.0 * mu_ref), (BATCH, LANES))
    inv_mu = jnp.broadcast_to(1.0 / (mu_ref * (GRID * PLANE)), (BATCH, LANES))

    for comp in range(6):
        value = jnp.concatenate([acc[comp]] * 2, axis=0)

        def start(pair, carry):
            for half in range(2):
                field[half, pl.ds(comp * block + pair * 16, 16), :] = value
            return carry

        lax.fori_loop(0, GRID // 2, start, 0)

    def prepare(pair, carry):
        for half in range(2):
            load = lambda row: rec[half, pl.ds(row * block + pair * 16, 16), :]
            level, mu, sat, rate = load(6), load(7), load(10), load(11)
            decay = jnp.exp(-rate * level)
            rec[half, pl.ds(12 * block + pair * 16, 16), :] = (
                load(9) + sat * (1.0 - decay) + SLOPE * level
            )
            rest = sat * decay
            rec[half, pl.ds(13 * block + pair * 16, 16), :] = rest
            rec[half, pl.ds(14 * block + pair * 16, 16), :] = 1.0 / (
                3.0 * mu + rest * rate + SLOPE
            )
        return carry

    lax.fori_loop(0, GRID // 2, prepare, 0)

    rm_pair = jnp.concatenate([rm_count] * 2, axis=0)
    second, third = rm_pair > 1, rm_pair > 2

    def newton(over, inc, mu3, rest, rate):
        decay = jnp.exp(-rate * inc)
        num = over - mu3 * inc - rest * (1.0 - decay)
        return inc + num / (mu3 + rest * rate * decay)

    def trial(half, pair):
        load = lambda row: rec[half, pl.ds(row * block + pair * 16, 16), :]
        elastic = [
            field[half, pl.ds(comp * block + pair * 16, 16), :] - load(comp) for comp in range(6)
        ]
        volume = elastic[0] + elastic[1] + elastic[2]
        mu = load(7)
        mu2 = 2.0 * mu
        mean = volume * (1.0 / 3.0)
        dev = [mu2 * (part - mean) for part in elastic[:3]] + [mu2 * part for part in elastic[3:]]
        squared = 1.5 * (dev[0] * dev[0] + dev[1] * dev[1] + dev[2] * dev[2]) + 3.0 * (
            dev[3] * dev[3] + dev[4] * dev[4] + dev[5] * dev[5]
        )
        return load, volume, mu, dev, squared

    def increments(load, mu, over):
        mu3 = 3.0 * mu + SLOPE
        rest, rate = load(13), load(11)
        inc = over * load(14)
        inc = jnp.where(second, newton(over, inc, mu3, rest, rate), inc)
        return jnp.where(third, newton(over, inc, mu3, rest, rate), inc)

    def stress_step(pair, carry):
        for half in range(2):
            load, volume, mu, dev, squared = trial(half, pair)
            base = load(9)
            capped = jnp.maximum(squared, base * base)
            inv_eq = lax.rsqrt(capped)
            over = jnp.maximum(capped * inv_eq - load(12), 0.0)
            inc = increments(load, mu, over)
            shrink = 1.0 - 3.0 * mu * inc * inv_eq
            pressure = load(8) * volume
            for comp in range(6):
                value = shrink * dev[comp]
                if comp < 3:
                    value = value + pressure
                upper = value.astype(jnp.bfloat16)
                at = pl.ds(comp * block + pair * 16, 16)
                lanes = slice(half * LANES, (half + 1) * LANES)
                part_hi[at, lanes] = upper
                part_lo[at, lanes] = (value - upper.astype(jnp.float32)).astype(jnp.bfloat16)
        return carry

    def plane_product(store):
        for which, (from_row, rows) in enumerate(
            ((0, 3 * block), (3 * block, block), (4 * block, block), (5 * block, block))
        ):
            for at in range(from_row, from_row + rows, block):
                left_hi = part_hi[at : at + block, :]
                left_lo = part_lo[at : at + block, :]
                dot = functools.partial(jnp.dot, preferred_element_type=jnp.float32)
                store(
                    at,
                    dot(left_hi, high[which])
                    + (dot(left_lo, high[which]) + dot(left_hi, low[which])),
                )

    def store_spec(at, value):
        for half in range(2):
            work[half, at : at + block, :] = value[:, half * LANES : (half + 1) * LANES]

    def update_field(at, value):
        for half in range(2):
            field[half, at : at + block, :] = (
                field[half, at : at + block, :] - value[:, half * LANES : (half + 1) * LANES]
            )

    def flip(comp, k):
        return (-k) % GRID if comp in (4, 5) else k

    def sweep(index, carry):
        lax.fori_loop(0, GRID // 2, stress_step, 0)
        plane_product(store_spec)
        scale_cell = jnp.where(index < fft_count, inv_mu, 0.0)

        def spectral(half, inner):
            for comp in range(6):
                lines = hartley(
                    [
                        work[half, comp * block + x * BATCH : comp * block + (x + 1) * BATCH, :]
                        for x in range(GRID)
                    ]
                )
                for k in range(GRID):
                    at = comp * block + flip(comp, k) * BATCH
                    spec[half, at : at + BATCH, :] = lines[k]
            wave_y = jnp.broadcast_to(table[half, GRID : GRID + 1, :], (BATCH, LANES))
            wave_z = jnp.broadcast_to(table[half, GRID + 1 : GRID + 2, :], (BATCH, LANES))
            for k in range(GRID):
                wave_x = waves[k]
                inv_sq = jnp.broadcast_to(table[half, k : k + 1, :], (BATCH, LANES))
                s = [
                    spec[half, comp * block + k * BATCH : comp * block + (k + 1) * BATCH, :]
                    for comp in range(6)
                ]
                comp_a = s[0] * wave_x + s[5] * wave_y + s[4] * wave_z
                comp_b = s[5] * wave_x + s[1] * wave_y + s[3] * wave_z
                comp_c = s[4] * wave_x + s[3] * wave_y + s[2] * wave_z
                along = (wave_x * comp_a + wave_y * comp_b + wave_z * comp_c) * (
                    inv_sq * coupling
                )
                scale = inv_sq * scale_cell
                vec_a = (comp_a - along * wave_x) * scale
                vec_b = (comp_b - along * wave_y) * scale
                vec_c = (comp_c - along * wave_z) * scale
                mapped = (
                    wave_x * vec_a,
                    wave_y * vec_b,
                    wave_z * vec_c,
                    0.5 * (wave_y * vec_c + wave_z * vec_b),
                    0.5 * (wave_x * vec_c + wave_z * vec_a),
                    0.5 * (wave_x * vec_b + wave_y * vec_a),
                )
                for comp in range(6):
                    at = comp * block + flip(comp, k) * BATCH
                    work[half, at : at + BATCH, :] = mapped[comp]
            return inner

        for half in range(2):
            spectral(half, 0)
            for comp in range(6):
                lines = hartley(
                    [
                        work[half, comp * block + x * BATCH : comp * block + (x + 1) * BATCH, :]
                        for x in range(GRID)
                    ]
                )
                for pair in range(GRID // 2):
                    value = jnp.concatenate([lines[2 * pair], lines[2 * pair + 1]], axis=0)
                    upper = value.astype(jnp.bfloat16)
                    at = comp * block + pair * 16
                    lanes = slice(half * LANES, (half + 1) * LANES)
                    part_hi[at : at + 16, lanes] = upper
                    part_lo[at : at + 16, lanes] = (value - upper.astype(jnp.float32)).astype(
                        jnp.bfloat16
                    )
        plane_product(update_field)
        return carry

    lax.fori_loop(0, most, sweep, 0)

    acc[...] = jnp.zeros_like(acc)

    def finish(pair, carry):
        for half in range(2):
            load, volume, mu, dev, squared = trial(half, pair)
            base = load(9)
            trial_eq = jnp.sqrt(squared)
            excess = trial_eq - load(12)
            over = jnp.maximum(excess, 0.0)
            inc = increments(load, mu, over)
            inv_eq = 1.0 / jnp.maximum(trial_eq, base)
            lost = 3.0 * mu * inc * inv_eq
            shrink = 1.0 - lost
            pressure = load(8) * volume
            grow = 1.5 * inc * inv_eq
            for comp in range(6):
                work[half, pl.ds(comp * block + pair * 16, 16), :] = load(comp) + grow * dev[comp]
            spec[half, pl.ds(pair * 16, 16), :] = load(6) + inc
            rate = load(11)
            slope = load(13) * rate * jnp.exp(-rate * inc) + SLOPE
            corr = jnp.where(excess > 0.0, 3.0 * mu / (3.0 * mu + slope) - lost, 0.0)
            weight = 3.0 * mu * corr * (inv_eq * inv_eq)
            terms = [shrink * part for part in dev]
            terms = [term + pressure for term in terms[:3]] + terms[3:]
            terms.append(load(8))
            terms.append(2.0 * mu * shrink)
            for c in range(6):
                scaled = weight * dev[c]
                for d in range(c, 6):
                    terms.append(scaled * dev[d])
            for at, term in enumerate(terms):
                acc[at] = acc[at] + (term[:BATCH] + term[BATCH:])
        return carry

    lax.fori_loop(0, GRID // 2, finish, 0)

    lane_of = lax.broadcasted_iota(jnp.int32, (BATCH, LANES), 1)
    out = jnp.zeros((BATCH, LANES), jnp.float32)
    for at in range(SUMS):
        out = jnp.where(lane_of == at, jnp.sum(acc[at], axis=1, keepdims=True), out)
    sums[...] = out * (1.0 / (GRID * PLANE))

    ahead = max(begin - first, 0)
    if begin:
        for at in range(ahead):
            after[at] = other[at]
    for slot in range(min(BATCH, total - begin)):
        alone = begin == 0 and slot < first
        target = other if alone else after
        here = slot if alone else begin + slot - first
        for half in range(2):
            for part in range(2):
                near = part * 16 + half
                for row in range(7):
                    source, from_row = (work, row) if row < 6 else (spec, 0)
                    at = (0 if alone else P_ROWS) + row * LINES + near
                    target[here, pl.ds(at, 8, stride=2), :] = source[
                        half, pl.ds(from_row * block + part * 64 + slot, 8, stride=BATCH), :
                    ]
                if not alone:
                    for row in range(5):
                        target[here, pl.ds(row * LINES + near, 8, stride=2), :] = rec[
                            half, pl.ds((7 + row) * block + part * 64 + slot, 8, stride=BATCH), :
                        ]


def merge_kernel(
    elems,
    points,
    first,
    order,
    s_head,
    rem,
    got_p,
    got_s,
    shear,
    bulk,
    base,
    sat,
    rate,
    new_state,
    new_props,
    cells,
    s_out,
    p_out,
    in_sem,
    own_sem,
    out_sem,
):
    total = elems * points
    moving = order[total]
    rows = LINES * points
    state_part = pl.ds(P_ROWS, S_ROWS)

    def own_props(e_at):
        return [
            pltpu.make_async_copy(
                source.at[pl.ds(pl.multiple_of(e_at * rows, 8), rows), :],
                p_out.at[e_at, pl.ds(row * rows, rows), :],
                own_sem.at[e_at],
            )
            for row, source in enumerate((shear, bulk, base, sat, rate))
        ]

    def arrival(cell, act):
        slot = order[total + 1 + cell]
        late = jnp.maximum(slot - first, 0)
        sem = in_sem.at[cell]
        moved, soon = slot < moving, slot < first

        @pl.when(jnp.logical_not(moved) & soon)
        def _():
            act(
                pltpu.make_async_copy(
                    s_head.at[jnp.minimum(slot, first - 1)], cells.at[cell, state_part, :], sem
                )
            )

        @pl.when(jnp.logical_not(soon))
        def _():
            act(pltpu.make_async_copy(rem.at[late], cells.at[cell], sem))

    def leaving(e_at):
        return (
            pltpu.make_async_copy(s_out.at[e_at], new_state.at[e_at], out_sem.at[e_at, 0]),
            pltpu.make_async_copy(p_out.at[e_at], new_props.at[e_at], out_sem.at[e_at, 1]),
        )

    @pl.loop(0, elems)
    def _(e_at):
        for g_at in range(points):
            arrival(e_at * points + g_at, lambda copy: copy.start())
        for copy in own_props(e_at):
            copy.start()

    @pl.loop(0, elems)
    def _(e_at):
        for copy in own_props(e_at):
            copy.wait()

        @pl.loop(0, points)
        def _(g_at):
            cell = e_at * points + g_at
            slot = order[total + 1 + cell]
            arrival(cell, lambda copy: copy.wait())
            moved, soon = slot < moving, slot < first
            early = jnp.minimum(slot, first - 1)

            def put(target, count, load):
                for row in range(count):
                    for part in range(0, LINES, 8):
                        at = row * rows + part * points + g_at
                        target[e_at, pl.ds(at, 8, stride=points), :] = load(row * LINES + part)

            @pl.when(moved & soon)
            def _():
                put(p_out, 5, lambda at: got_p[early, at : at + 8, :])
                put(s_out, 7, lambda at: got_s[early, at : at + 8, :])

            @pl.when(moved & jnp.logical_not(soon))
            def _():
                put(p_out, 5, lambda at: cells[cell, at : at + 8, :])

            @pl.when(jnp.logical_not(moved & soon))
            def _():
                put(s_out, 7, lambda at: cells[cell, P_ROWS + at : P_ROWS + at + 8, :])

        for copy in leaving(e_at):
            copy.start()

    @pl.loop(0, elems)
    def _(e_at):
        for copy in leaving(e_at):
            copy.wait()


def element_terms(table_part, sums, points):
    elems = sums.shape[0] // points
    weights = np.array([1.0, 1.0, 1.0, 2.0, 2.0, 2.0], np.float32)
    stress = sums[:, 0:6]
    block = np.outer([1.0, 1.0, 1.0, 0.0, 0.0, 0.0], [1.0, 1.0, 1.0, 0.0, 0.0, 0.0])
    spread = np.zeros((23, 36), np.float32)
    spread[0] = block.reshape(36)
    spread[1] = (np.eye(6) - block / 3.0).reshape(36)
    at = 2
    for c in range(6):
        for d in range(c, 6):
            spread[at, 6 * c + d] = -weights[d]
            spread[at, 6 * d + c] = -weights[c]
            at += 1
    tangent = jnp.dot(sums[:, 6:SUMS], spread, precision=top_precision)
    stress_part = stress.reshape(elems, points, 6)
    force = (
        jnp.einsum("egc,gcn->en", stress_part * weights, table_part, precision=top_precision)
        / GAUSS
    )
    scaled = tangent.reshape(elems, points, 6, 6) * weights[None, None, :, None]
    stiff = (
        jnp.einsum(
            "gcn,egcd,gdm->enm", table_part, scaled, table_part, precision=top_precision
        ).reshape(elems, 576)
        / GAUSS
    )
    return stress_part, force, stiff


VMEM = pl.BlockSpec(memory_space=pltpu.VMEM)
SMEM = pl.BlockSpec(memory_space=pltpu.SMEM)
ANY = pl.BlockSpec(memory_space=pl.ANY)
GRANT = 60 * 2**20
MERGE_GRANT = 24 * 2**20


def shape(*dims, dtype=jnp.float32):
    return jax.ShapeDtypeStruct(dims, dtype)


def local(
    elem_disp,
    plastic_strain,
    hardening_var,
    shear_mod,
    bulk_mod,
    yield_stress,
    sat_stress,
    sat_rate,
    fft_iters,
    rm_iters,
    move_flag,
):
    elems, points = plastic_strain.shape[:2]
    voxels = plastic_strain.shape[3]
    total = elems * points
    group = min(BATCH, total)
    first = max(1, total * EARLY // 16)
    devices = lax.axis_size("cell")
    route = [((i - devices // 2) % devices, i) for i in range(devices)]

    params = pltpu.CompilerParams(vmem_limit_bytes=GRANT)
    bmat = jnp.asarray(strain_table())

    def flat(array):
        lead = array.shape[2:-1]
        tiles = array.reshape(elems, points, *lead, LINES, LANES)
        return jnp.moveaxis(tiles, 1, -2).reshape(-1, LANES)

    def whole(lines, lead):
        tiles = lines.reshape(elems, lead, LINES, points, LANES)
        return jnp.moveaxis(tiles, 3, 1).reshape(elems, points, lead, voxels)

    props = [flat(a) for a in (shear_mod, bulk_mod, yield_stress, sat_stress, sat_rate)]
    hard, plastic = flat(hardening_var), flat(plastic_strain)
    order, p_head = pl.pallas_call(
        functools.partial(pack_kernel, elems, points, first),
        out_shape=(shape(2 * total + 1, dtype=jnp.int32), shape(first, P_ROWS, LANES)),
        in_specs=[SMEM] + [VMEM] * 5,
        out_specs=(SMEM, VMEM),
        compiler_params=params,
        name="pack",
    )(move_flag, *props)

    got_p = lax.ppermute(p_head, "cell", route)

    high, low, table, waves = cas_tables()
    table = table.reshape(24, 2, LANES).transpose(1, 0, 2)
    block = GRID * BATCH
    disp = elem_disp.reshape(elems, 1, elem_disp.shape[1])

    def solve(begin, count, other=None):
        late = shape(count, ROWS, LANES)
        alone = () if begin else (shape(first, S_ROWS, LANES),)
        return pl.pallas_call(
            functools.partial(solve_kernel, elems, points, begin, first, waves),
            out_shape=alone + (late, shape(BATCH, LANES)),
            in_specs=[SMEM] * 3 + [VMEM] * (13 if begin else 12),
            out_specs=(VMEM,) * (len(alone) + 2),
            scratch_shapes=[
                pltpu.VMEM((2, 15 * block, LANES), jnp.float32),
                pltpu.VMEM((2, 6 * block, LANES), jnp.float32),
                pltpu.VMEM((2, 6 * block, LANES), jnp.float32),
                pltpu.VMEM((2, 6 * block, LANES), jnp.float32),
                pltpu.VMEM((6 * block, PLANE), jnp.bfloat16),
                pltpu.VMEM((6 * block, PLANE), jnp.bfloat16),
                pltpu.VMEM((SUMS, BATCH, LANES), jnp.float32),
            ],
            compiler_params=params,
            cost_estimate=pl.CostEstimate(
                flops=20 * 10**9, bytes_accessed=8 * 10**6, transcendentals=0
            ),
            name="solve",
        )(
            order,
            fft_iters,
            rm_iters,
            disp,
            bmat,
            plastic,
            hard,
            *props,
            high,
            low,
            table,
            *(() if other is None else (other,)),
        )

    s_head, rem, sums = solve(0, group - first)
    got_s = lax.ppermute(s_head, "cell", route)
    if total > group:
        rem, more = solve(group, total - first, rem)
        sums = jnp.concatenate([sums, more], axis=0)

    slots = order[:total]
    place = (slots[None, :] == jnp.arange(total)[:, None]).astype(jnp.float32)
    sums = jnp.dot(place, sums[:total], precision=top_precision)
    table_part = lax.dynamic_slice_in_dim(bmat, lax.axis_index("sec") * points, points, 0)
    stress, force_part, stiff_part = element_terms(table_part, sums, points)
    sections = lax.axis_size("sec")
    force, stiff = force_part, stiff_part
    for step in range(1, sections):
        ring = [((i - step) % sections, i) for i in range(sections)]
        force = force + lax.ppermute(force_part, "sec", ring)
        stiff = stiff + lax.ppermute(stiff_part, "sec", ring)
    rem, force, stiff, stress = lax.optimization_barrier((rem, force, stiff, stress))

    def branch(count):
        def run(cells):
            if count == 0:
                return cells
            got = lax.ppermute(cells[:count], "cell", route)
            return lax.dynamic_update_slice_in_dim(cells, got, 0, 0)

        return run

    extra = jnp.clip(
        jnp.sum((move_flag > 0).astype(jnp.int32)) - first, 0, total - first
    )
    rem = lax.switch(extra, [branch(c) for c in range(total - first + 1)], rem)

    new_state, new_props = pl.pallas_call(
        functools.partial(merge_kernel, elems, points, first),
        out_shape=(
            shape(elems, 7 * LINES * points, LANES),
            shape(elems, 5 * LINES * points, LANES),
        ),
        in_specs=[SMEM] + [ANY] * 2 + [VMEM] * 2 + [ANY] * 5,
        out_specs=(ANY, ANY),
        scratch_shapes=[
            pltpu.VMEM((total, ROWS, LANES), jnp.float32),
            pltpu.VMEM((elems, 7 * LINES * points, LANES), jnp.float32),
            pltpu.VMEM((elems, 5 * LINES * points, LANES), jnp.float32),
            pltpu.SemaphoreType.DMA((total,)),
            pltpu.SemaphoreType.DMA((elems,)),
            pltpu.SemaphoreType.DMA((elems, 2)),
        ],
        compiler_params=pltpu.CompilerParams(vmem_limit_bytes=MERGE_GRANT),
        name="merge",
    )(order, s_head, rem, got_p, got_s, *props)
    return force, stiff, stress, whole(new_state, 7), whole(new_props, 5)


def solution(mesh):
    in_specs = (
        P("cell", None),
        P("cell", "sec", None, None),
        P("cell", "sec", None),
        P("cell", "sec", None),
        P("cell", "sec", None),
        P("cell", "sec", None),
        P("cell", "sec", None),
        P("cell", "sec", None),
        P("cell", "sec"),
        P("cell", "sec"),
        P("cell", "sec"),
    )
    out_specs = (
        P("cell", None),
        P("cell", None),
        P("cell", "sec", None),
        P("cell", "sec", None, None),
        P("cell", "sec", None, None),
    )

    return jax.shard_map(local, mesh=mesh, in_specs=in_specs, out_specs=out_specs, check_vma=False)
```

```python
import functools
import math

import jax
import jax.numpy as jnp
import numpy as np
from jax import lax
from jax.experimental import pallas as pl
from jax.experimental.pallas import tpu as pltpu
from jax.sharding import PartitionSpec as P


GRID = 16
PLANE = GRID * GRID
LANES = 128
BATCH = 8
GAUSS = 8
SLOPE = 0.05
top_precision = lax.Precision.HIGHEST
SUMS = 29
LINES = GRID * PLANE // LANES
P_ROWS = 5 * LINES
S_ROWS = 7 * LINES
ROWS = P_ROWS + S_ROWS
EARLY = 6


def strain_table():
    root = 1.0 / math.sqrt(3.0)
    table = np.zeros((8, 6, 24), np.float32)
    for gauss_pt in range(8):
        point = [((gauss_pt >> axis_bit & 1) * 2 - 1) * root for axis_bit in range(3)]
        for node in range(8):
            signs = [(node >> axis_bit & 1) * 2 - 1 for axis_bit in range(3)]
            grads = []
            for axis_bit in range(3):
                factor = 2.0 * signs[axis_bit] / 8.0
                for other in range(3):
                    if other != axis_bit:
                        factor = factor * (1.0 + signs[other] * point[other])
                grads.append(factor)
            table[gauss_pt, 0, 3 * node + 0] = grads[0]
            table[gauss_pt, 1, 3 * node + 1] = grads[1]
            table[gauss_pt, 2, 3 * node + 2] = grads[2]
            table[gauss_pt, 3, 3 * node + 1] = 0.5 * grads[2]
            table[gauss_pt, 3, 3 * node + 2] = 0.5 * grads[1]
            table[gauss_pt, 4, 3 * node + 0] = 0.5 * grads[2]
            table[gauss_pt, 4, 3 * node + 2] = 0.5 * grads[0]
            table[gauss_pt, 5, 3 * node + 0] = 0.5 * grads[1]
            table[gauss_pt, 5, 3 * node + 1] = 0.5 * grads[0]
    return table


def cas_tables():
    index = np.arange(GRID)
    angle = 2.0 * np.pi * (np.outer(index, index) % GRID) / GRID
    plus = np.cos(angle) + np.sin(angle)
    minus = np.cos(angle) - np.sin(angle)
    full = np.stack(
        [np.kron(plus, plus), -np.kron(minus, minus), -np.kron(plus, minus), -np.kron(minus, plus)]
    ).astype(np.float32)
    high = full.astype(jnp.bfloat16)
    low = (full - high.astype(np.float32)).astype(jnp.bfloat16)
    waves = np.sin(2.0 * np.pi * index / GRID)
    wave_y = np.repeat(waves, GRID)
    wave_z = np.tile(waves, GRID)
    squared = waves[:, None] ** 2 + wave_y[None, :] ** 2 + wave_z[None, :] ** 2
    inv_sq = np.where(squared > 0.01, 1.0 / np.maximum(squared, 0.01), 0.0)
    table = np.concatenate([inv_sq, wave_y[None], wave_z[None], np.zeros((6, PLANE))], axis=0)
    return high, low, table.astype(np.float32), [float(w) for w in waves]


def hartley(values):
    count = len(values)
    if count == 1:
        return list(values)
    half = count // 2
    even = hartley(values[0::2])
    odd = hartley(values[1::2])
    low, high = [], []
    for k in range(half):
        other = odd[(-k) % half]
        if k == 0:
            term = odd[0]
        elif 4 * k == count:
            term = other
        elif 8 * k == count:
            term = (odd[k] + other) * math.sqrt(0.5)
        elif 8 * k == 3 * count:
            term = (other - odd[k]) * math.sqrt(0.5)
        else:
            turn = 2.0 * math.pi * k / count
            term = odd[k] * math.cos(turn) + other * math.sin(turn)
        low.append(even[k] + term)
        high.append(even[k] - term)
    return low + high


def pack_kernel(elems, points, first, flag, *refs):
    *sources, order, head = refs
    total = elems * points

    def place(wanted, start):
        def step(cell, at):
            hit = (flag[cell // points, cell % points] > 0) == wanted

            @pl.when(hit)
            def _():
                order[at] = cell
                order[total + 1 + cell] = at

            return at + hit.astype(jnp.int32)

        return lax.fori_loop(0, total, step, start)

    moving = place(True, jnp.int32(0))
    place(False, moving)
    order[total] = moving

    for slot in range(first):
        cell = order[slot]
        at = (cell // points) * (LINES * points) + cell % points
        for row, source in enumerate(sources):
            for part in range(0, LINES, 8):
                head[slot, row * LINES + part : row * LINES + part + 8, :] = source[
                    pl.ds(at + part * points, 8, stride=points), :
                ]


def solve_kernel(
    elems,
    points,
    begin,
    first,
    waves,
    order,
    fft_iters,
    rm_iters,
    disp,
    bmat,
    plastic,
    hard,
    shear,
    bulk,
    base,
    sat,
    rate,
    high,
    low,
    table,
    other,
    after,
    sums,
    rec,
    field,
    work,
    spec,
    part_hi,
    part_lo,
    acc,
):
    total = elems * points
    block = GRID * BATCH
    row_of = lax.broadcasted_iota(jnp.int32, (BATCH, LANES), 0)

    cells = [order[min(begin + slot, total - 1)] for slot in range(BATCH)]

    section = lax.axis_index("sec")

    def fill(slot, carry):
        cell = order[jnp.minimum(begin + slot, total - 1)]
        e_at, g_at = cell // points, cell % points
        for half in range(2):
            for part in range(2):
                near = (part * 16 + half) * points + g_at
                here = part * 64 + slot
                for comp in range(6):
                    at = (e_at * 6 + comp) * (LINES * points) + near
                    rec[half, pl.ds(comp * block + here, 8, stride=BATCH), :] = plastic[
                        pl.ds(at, 8, stride=2 * points), :
                    ]
                for row, source in enumerate((hard, shear, bulk, base, sat, rate)):
                    at = e_at * (LINES * points) + near
                    rec[half, pl.ds((6 + row) * block + here, 8, stride=BATCH), :] = source[
                        pl.ds(at, 8, stride=2 * points), :
                    ]
        value = jnp.sum(bmat[section * points + g_at] * disp[e_at], axis=1, keepdims=True)
        acc[pl.ds(0, 6), pl.ds(slot, 1), :] = jnp.broadcast_to(value, (6, LANES))[:, None, :]
        return carry

    lax.fori_loop(0, BATCH, fill, 0)

    def per_cell(pick, dtype):
        out = jnp.zeros((BATCH, LANES), dtype)
        for slot in range(BATCH):
            out = jnp.where(row_of == slot, pick(slot), out)
        return out

    fft_count = per_cell(lambda s: fft_iters[cells[s] // points, cells[s] % points], jnp.int32)
    rm_count = per_cell(lambda s: rm_iters[cells[s] // points, cells[s] % points], jnp.int32)
    most = functools.reduce(
        jnp.maximum, [fft_iters[c // points, c % points] for c in cells]
    )

    def extremes(row):
        top = bottom = None
        for half in range(2):
            for x in range(GRID):
                value = rec[half, row * block + x * BATCH : row * block + (x + 1) * BATCH, :]
                top = value if top is None else jnp.maximum(top, value)
                bottom = value if bottom is None else jnp.minimum(bottom, value)
        return 0.5 * (
            jnp.max(top, axis=1, keepdims=True) + jnp.min(bottom, axis=1, keepdims=True)
        )

    mu_ref = extremes(7)
    bulk_ref = extremes(8)
    lame_ref = bulk_ref - 2.0 * mu_ref / 3.0
    coupling = jnp.broadcast_to((lame_ref + mu_ref) / (lame_ref + 2.0 * mu_ref), (BATCH, LANES))
    inv_mu = jnp.broadcast_to(1.0 / (mu_ref * (GRID * PLANE)), (BATCH, LANES))

    for comp in range(6):
        value = jnp.concatenate([acc[comp]] * 2, axis=0)

        def start(pair, carry):
            for half in range(2):
                field[half, pl.ds(comp * block + pair * 16, 16), :] = value
            return carry

        lax.fori_loop(0, GRID // 2, start, 0)

    def prepare(pair, carry):
        for half in range(2):
            load = lambda row: rec[half, pl.ds(row * block + pair * 16, 16), :]
            level, mu, sat, rate = load(6), load(7), load(10), load(11)
            decay = jnp.exp(-rate * level)
            rec[half, pl.ds(12 * block + pair * 16, 16), :] = (
                load(9) + sat * (1.0 - decay) + SLOPE * level
            )
            rest = sat * decay
            rec[half, pl.ds(13 * block + pair * 16, 16), :] = rest
            rec[half, pl.ds(14 * block + pair * 16, 16), :] = 1.0 / (
                3.0 * mu + rest * rate + SLOPE
            )
        return carry

    lax.fori_loop(0, GRID // 2, prepare, 0)

    rm_pair = jnp.concatenate([rm_count] * 2, axis=0)
    second, third = rm_pair > 1, rm_pair > 2

    def newton(over, inc, mu3, rest, rate):
        decay = jnp.exp(-rate * inc)
        num = over - mu3 * inc - rest * (1.0 - decay)
        return inc + num / (mu3 + rest * rate * decay)

    def trial(half, pair):
        load = lambda row: rec[half, pl.ds(row * block + pair * 16, 16), :]
        elastic = [
            field[half, pl.ds(comp * block + pair * 16, 16), :] - load(comp) for comp in range(6)
        ]
        volume = elastic[0] + elastic[1] + elastic[2]
        mu = load(7)
        mu2 = 2.0 * mu
        mean = volume * (1.0 / 3.0)
        dev = [mu2 * (part - mean) for part in elastic[:3]] + [mu2 * part for part in elastic[3:]]
        squared = 1.5 * (dev[0] * dev[0] + dev[1] * dev[1] + dev[2] * dev[2]) + 3.0 * (
            dev[3] * dev[3] + dev[4] * dev[4] + dev[5] * dev[5]
        )
        return load, volume, mu, dev, squared

    def increments(load, mu, over):
        mu3 = 3.0 * mu + SLOPE
        rest, rate = load(13), load(11)
        inc = over * load(14)
        inc = jnp.where(second, newton(over, inc, mu3, rest, rate), inc)
        return jnp.where(third, newton(over, inc, mu3, rest, rate), inc)

    def stress_step(pair, carry):
        for half in range(2):
            load, volume, mu, dev, squared = trial(half, pair)
            base = load(9)
            capped = jnp.maximum(squared, base * base)
            inv_eq = lax.rsqrt(capped)
            over = jnp.maximum(capped * inv_eq - load(12), 0.0)
            inc = increments(load, mu, over)
            shrink = 1.0 - 3.0 * mu * inc * inv_eq
            pressure = load(8) * volume
            for comp in range(6):
                value = shrink * dev[comp]
                if comp < 3:
                    value = value + pressure
                upper = value.astype(jnp.bfloat16)
                at = pl.ds(comp * block + pair * 16, 16)
                lanes = slice(half * LANES, (half + 1) * LANES)
                part_hi[at, lanes] = upper
                part_lo[at, lanes] = (value - upper.astype(jnp.float32)).astype(jnp.bfloat16)
        return carry

    def plane_product(store):
        for which, (from_row, rows) in enumerate(
            ((0, 3 * block), (3 * block, block), (4 * block, block), (5 * block, block))
        ):
            for at in range(from_row, from_row + rows, block):
                left_hi = part_hi[at : at + block, :]
                left_lo = part_lo[at : at + block, :]
                dot = functools.partial(jnp.dot, preferred_element_type=jnp.float32)
                store(
                    at,
                    dot(left_hi, high[which])
                    + (dot(left_lo, high[which]) + dot(left_hi, low[which])),
                )

    def store_spec(at, value):
        for half in range(2):
            work[half, at : at + block, :] = value[:, half * LANES : (half + 1) * LANES]

    def update_field(at, value):
        for half in range(2):
            field[half, at : at + block, :] = (
                field[half, at : at + block, :] - value[:, half * LANES : (half + 1) * LANES]
            )

    def flip(comp, k):
        return (-k) % GRID if comp in (4, 5) else k

    def sweep(index, carry):
        lax.fori_loop(0, GRID // 2, stress_step, 0)
        plane_product(store_spec)
        scale_cell = jnp.where(index < fft_count, inv_mu, 0.0)

        def spectral(half, inner):
            for comp in range(6):
                lines = hartley(
                    [
                        work[half, comp * block + x * BATCH : comp * block + (x + 1) * BATCH, :]
                        for x in range(GRID)
                    ]
                )
                for k in range(GRID):
                    at = comp * block + flip(comp, k) * BATCH
                    spec[half, at : at + BATCH, :] = lines[k]
            wave_y = jnp.broadcast_to(table[half, GRID : GRID + 1, :], (BATCH, LANES))
            wave_z = jnp.broadcast_to(table[half, GRID + 1 : GRID + 2, :], (BATCH, LANES))
            for k in range(GRID):
                wave_x = waves[k]
                inv_sq = jnp.broadcast_to(table[half, k : k + 1, :], (BATCH, LANES))
                s = [
                    spec[half, comp * block + k * BATCH : comp * block + (k + 1) * BATCH, :]
                    for comp in range(6)
                ]
                comp_a = s[0] * wave_x + s[5] * wave_y + s[4] * wave_z
                comp_b = s[5] * wave_x + s[1] * wave_y + s[3] * wave_z
                comp_c = s[4] * wave_x + s[3] * wave_y + s[2] * wave_z
                along = (wave_x * comp_a + wave_y * comp_b + wave_z * comp_c) * (
                    inv_sq * coupling
                )
                scale = inv_sq * scale_cell
                vec_a = (comp_a - along * wave_x) * scale
                vec_b = (comp_b - along * wave_y) * scale
                vec_c = (comp_c - along * wave_z) * scale
                mapped = (
                    wave_x * vec_a,
                    wave_y * vec_b,
                    wave_z * vec_c,
                    0.5 * (wave_y * vec_c + wave_z * vec_b),
                    0.5 * (wave_x * vec_c + wave_z * vec_a),
                    0.5 * (wave_x * vec_b + wave_y * vec_a),
                )
                for comp in range(6):
                    at = comp * block + flip(comp, k) * BATCH
                    work[half, at : at + BATCH, :] = mapped[comp]
            return inner

        for half in range(2):
            spectral(half, 0)
            for comp in range(6):
                lines = hartley(
                    [
                        work[half, comp * block + x * BATCH : comp * block + (x + 1) * BATCH, :]
                        for x in range(GRID)
                    ]
                )
                for pair in range(GRID // 2):
                    value = jnp.concatenate([lines[2 * pair], lines[2 * pair + 1]], axis=0)
                    upper = value.astype(jnp.bfloat16)
                    at = comp * block + pair * 16
                    lanes = slice(half * LANES, (half + 1) * LANES)
                    part_hi[at : at + 16, lanes] = upper
                    part_lo[at : at + 16, lanes] = (value - upper.astype(jnp.float32)).astype(
                        jnp.bfloat16
                    )
        plane_product(update_field)
        return carry

    lax.fori_loop(0, most, sweep, 0)

    acc[...] = jnp.zeros_like(acc)

    def finish(pair, carry):
        for half in range(2):
            load, volume, mu, dev, squared = trial(half, pair)
            base = load(9)
            trial_eq = jnp.sqrt(squared)
            excess = trial_eq - load(12)
            over = jnp.maximum(excess, 0.0)
            inc = increments(load, mu, over)
            inv_eq = 1.0 / jnp.maximum(trial_eq, base)
            lost = 3.0 * mu * inc * inv_eq
            shrink = 1.0 - lost
            pressure = load(8) * volume
            grow = 1.5 * inc * inv_eq
            for comp in range(6):
                work[half, pl.ds(comp * block + pair * 16, 16), :] = load(comp) + grow * dev[comp]
            spec[half, pl.ds(pair * 16, 16), :] = load(6) + inc
            rate = load(11)
            slope = load(13) * rate * jnp.exp(-rate * inc) + SLOPE
            corr = jnp.where(excess > 0.0, 3.0 * mu / (3.0 * mu + slope) - lost, 0.0)
            weight = 3.0 * mu * corr * (inv_eq * inv_eq)
            terms = [shrink * part for part in dev]
            terms = [term + pressure for term in terms[:3]] + terms[3:]
            terms.append(load(8))
            terms.append(2.0 * mu * shrink)
            for c in range(6):
                scaled = weight * dev[c]
                for d in range(c, 6):
                    terms.append(scaled * dev[d])
            for at, term in enumerate(terms):
                acc[at] = acc[at] + (term[:BATCH] + term[BATCH:])
        return carry

    lax.fori_loop(0, GRID // 2, finish, 0)

    lane_of = lax.broadcasted_iota(jnp.int32, (BATCH, LANES), 1)
    out = jnp.zeros((BATCH, LANES), jnp.float32)
    for at in range(SUMS):
        out = jnp.where(lane_of == at, jnp.sum(acc[at], axis=1, keepdims=True), out)
    sums[...] = out * (1.0 / (GRID * PLANE))

    ahead = max(begin - first, 0)
    if begin:
        for at in range(ahead):
            after[at] = other[at]
    for slot in range(min(BATCH, total - begin)):
        alone = begin == 0 and slot < first
        target = other if alone else after
        here = slot if alone else begin + slot - first
        for half in range(2):
            for part in range(2):
                near = part * 16 + half
                for row in range(7):
                    source, from_row = (work, row) if row < 6 else (spec, 0)
                    at = (0 if alone else P_ROWS) + row * LINES + near
                    target[here, pl.ds(at, 8, stride=2), :] = source[
                        half, pl.ds(from_row * block + part * 64 + slot, 8, stride=BATCH), :
                    ]
                if not alone:
                    for row in range(5):
                        target[here, pl.ds(row * LINES + near, 8, stride=2), :] = rec[
                            half, pl.ds((7 + row) * block + part * 64 + slot, 8, stride=BATCH), :
                        ]


def merge_kernel(
    elems,
    points,
    first,
    order,
    rem,
    s_head,
    got_p,
    got_s,
    shear,
    bulk,
    base,
    sat,
    rate,
    new_state,
    new_props,
    cells,
    s_out,
    p_out,
    in_sem,
    out_sem,
):
    total = elems * points
    moving = order[total]
    rows = LINES * points

    def arrival(slot):
        late = slot - first
        return pltpu.make_async_copy(rem.at[late], cells.at[late], in_sem.at[late])

    def leaving(e_at):
        return (
            pltpu.make_async_copy(s_out.at[e_at], new_state.at[e_at], out_sem.at[e_at, 0]),
            pltpu.make_async_copy(p_out.at[e_at], new_props.at[e_at], out_sem.at[e_at, 1]),
        )

    def put(target, cell, count, load):
        for row in range(count):
            for part in range(0, LINES, 8):
                at = row * rows + part * points + cell % points
                target[cell // points, pl.ds(at, 8, stride=points), :] = load(row * LINES + part)

    @pl.loop(first, total)
    def _(slot):
        arrival(slot).start()

    @pl.loop(0, elems)
    def _(e_at):
        for row, source in enumerate((shear, bulk, base, sat, rate)):
            p_out[e_at, pl.ds(row * rows, rows), :] = source[
                pl.ds(pl.multiple_of(e_at * rows, rows), rows), :
            ]

    @pl.loop(0, first)
    def _(slot):
        cell = order[slot]

        @pl.when(slot < moving)
        def _():
            put(p_out, cell, 5, lambda at: got_p[slot, at : at + 8, :])
            put(s_out, cell, 7, lambda at: got_s[slot, at : at + 8, :])

        @pl.when(slot >= moving)
        def _():
            put(s_out, cell, 7, lambda at: s_head[slot, at : at + 8, :])

    @pl.loop(0, elems)
    def _(e_at):
        @pl.loop(0, points)
        def _(g_at):
            cell = e_at * points + g_at
            slot = order[total + 1 + cell]
            late = jnp.maximum(slot - first, 0)

            @pl.when(slot >= first)
            def _():
                arrival(jnp.maximum(slot, first)).wait()
                put(s_out, cell, 7, lambda at: cells[late, P_ROWS + at : P_ROWS + at + 8, :])

            @pl.when((slot >= first) & (slot < moving))
            def _():
                put(p_out, cell, 5, lambda at: cells[late, at : at + 8, :])

        for copy in leaving(e_at):
            copy.start()

    @pl.loop(0, elems)
    def _(e_at):
        for copy in leaving(e_at):
            copy.wait()


def element_terms(table_part, sums, points):
    elems = sums.shape[0] // points
    weights = np.array([1.0, 1.0, 1.0, 2.0, 2.0, 2.0], np.float32)
    stress = sums[:, 0:6]
    block = np.outer([1.0, 1.0, 1.0, 0.0, 0.0, 0.0], [1.0, 1.0, 1.0, 0.0, 0.0, 0.0])
    spread = np.zeros((23, 36), np.float32)
    spread[0] = block.reshape(36)
    spread[1] = (np.eye(6) - block / 3.0).reshape(36)
    at = 2
    for c in range(6):
        for d in range(c, 6):
            spread[at, 6 * c + d] = -weights[d]
            spread[at, 6 * d + c] = -weights[c]
            at += 1
    tangent = jnp.dot(sums[:, 6:SUMS], spread, precision=top_precision)
    stress_part = stress.reshape(elems, points, 6)
    force = (
        jnp.einsum("egc,gcn->en", stress_part * weights, table_part, precision=top_precision)
        / GAUSS
    )
    scaled = tangent.reshape(elems, points, 6, 6) * weights[None, None, :, None]
    stiff = (
        jnp.einsum(
            "gcn,egcd,gdm->enm", table_part, scaled, table_part, precision=top_precision
        ).reshape(elems, 576)
        / GAUSS
    )
    return stress_part, force, stiff


VMEM = pl.BlockSpec(memory_space=pltpu.VMEM)
SMEM = pl.BlockSpec(memory_space=pltpu.SMEM)
ANY = pl.BlockSpec(memory_space=pl.ANY)
GRANT = 60 * 2**20
MERGE_GRANT = 24 * 2**20


def shape(*dims, dtype=jnp.float32):
    return jax.ShapeDtypeStruct(dims, dtype)


def local(
    elem_disp,
    plastic_strain,
    hardening_var,
    shear_mod,
    bulk_mod,
    yield_stress,
    sat_stress,
    sat_rate,
    fft_iters,
    rm_iters,
    move_flag,
):
    elems, points = plastic_strain.shape[:2]
    voxels = plastic_strain.shape[3]
    total = elems * points
    group = min(BATCH, total)
    first = max(1, total * EARLY // 16)
    devices = lax.axis_size("cell")
    route = [((i - devices // 2) % devices, i) for i in range(devices)]

    params = pltpu.CompilerParams(vmem_limit_bytes=GRANT)
    bmat = jnp.asarray(strain_table())

    def flat(array):
        lead = array.shape[2:-1]
        tiles = array.reshape(elems, points, *lead, LINES, LANES)
        return jnp.moveaxis(tiles, 1, -2).reshape(-1, LANES)

    def whole(lines, lead):
        tiles = lines.reshape(elems, lead, LINES, points, LANES)
        return jnp.moveaxis(tiles, 3, 1).reshape(elems, points, lead, voxels)

    props = [flat(a) for a in (shear_mod, bulk_mod, yield_stress, sat_stress, sat_rate)]
    hard, plastic = flat(hardening_var), flat(plastic_strain)
    order, p_head = pl.pallas_call(
        functools.partial(pack_kernel, elems, points, first),
        out_shape=(shape(2 * total + 1, dtype=jnp.int32), shape(first, P_ROWS, LANES)),
        in_specs=[SMEM] + [VMEM] * 5,
        out_specs=(SMEM, VMEM),
        compiler_params=params,
        name="pack",
    )(move_flag, *props)

    got_p = lax.ppermute(p_head, "cell", route)

    high, low, table, waves = cas_tables()
    table = table.reshape(24, 2, LANES).transpose(1, 0, 2)
    block = GRID * BATCH
    disp = elem_disp.reshape(elems, 1, elem_disp.shape[1])

    def solve(begin, count, other=None):
        late = shape(count, ROWS, LANES)
        alone = () if begin else (shape(first, S_ROWS, LANES),)
        return pl.pallas_call(
            functools.partial(solve_kernel, elems, points, begin, first, waves),
            out_shape=alone + (late, shape(BATCH, LANES)),
            in_specs=[SMEM] * 3 + [VMEM] * (13 if begin else 12),
            out_specs=(VMEM,) * (len(alone) + 2),
            scratch_shapes=[
                pltpu.VMEM((2, 15 * block, LANES), jnp.float32),
                pltpu.VMEM((2, 6 * block, LANES), jnp.float32),
                pltpu.VMEM((2, 6 * block, LANES), jnp.float32),
                pltpu.VMEM((2, 6 * block, LANES), jnp.float32),
                pltpu.VMEM((6 * block, PLANE), jnp.bfloat16),
                pltpu.VMEM((6 * block, PLANE), jnp.bfloat16),
                pltpu.VMEM((SUMS, BATCH, LANES), jnp.float32),
            ],
            compiler_params=params,
            cost_estimate=pl.CostEstimate(
                flops=20 * 10**9, bytes_accessed=8 * 10**6, transcendentals=0
            ),
            name="solve",
        )(
            order,
            fft_iters,
            rm_iters,
            disp,
            bmat,
            plastic,
            hard,
            *props,
            high,
            low,
            table,
            *(() if other is None else (other,)),
        )

    s_head, rem, sums = solve(0, group - first)
    got_s = lax.ppermute(s_head, "cell", route)
    if total > group:
        rem, more = solve(group, total - first, rem)
        sums = jnp.concatenate([sums, more], axis=0)

    slots = order[:total]
    place = (slots[None, :] == jnp.arange(total)[:, None]).astype(jnp.float32)
    sums = jnp.dot(place, sums[:total], precision=top_precision)
    table_part = lax.dynamic_slice_in_dim(bmat, lax.axis_index("sec") * points, points, 0)
    stress, force_part, stiff_part = element_terms(table_part, sums, points)
    sections = lax.axis_size("sec")
    force, stiff = force_part, stiff_part
    for step in range(1, sections):
        ring = [((i - step) % sections, i) for i in range(sections)]
        force = force + lax.ppermute(force_part, "sec", ring)
        stiff = stiff + lax.ppermute(stiff_part, "sec", ring)
    rem, force, stiff, stress = lax.optimization_barrier((rem, force, stiff, stress))

    def branch(count):
        def run(cells):
            if count == 0:
                return cells
            got = lax.ppermute(cells[:count], "cell", route)
            return lax.dynamic_update_slice_in_dim(cells, got, 0, 0)

        return run

    extra = jnp.clip(
        jnp.sum((move_flag > 0).astype(jnp.int32)) - first, 0, total - first
    )
    rem = lax.switch(extra, [branch(c) for c in range(total - first + 1)], rem)

    new_state, new_props = pl.pallas_call(
        functools.partial(merge_kernel, elems, points, first),
        out_shape=(
            shape(elems, 7 * LINES * points, LANES),
            shape(elems, 5 * LINES * points, LANES),
        ),
        in_specs=[SMEM, ANY] + [VMEM] * 8,
        out_specs=(ANY, ANY),
        scratch_shapes=[
            pltpu.VMEM((total - first, ROWS, LANES), jnp.float32),
            pltpu.VMEM((elems, 7 * LINES * points, LANES), jnp.float32),
            pltpu.VMEM((elems, 5 * LINES * points, LANES), jnp.float32),
            pltpu.SemaphoreType.DMA((total - first,)),
            pltpu.SemaphoreType.DMA((elems, 2)),
        ],
        compiler_params=pltpu.CompilerParams(vmem_limit_bytes=MERGE_GRANT),
        name="merge",
    )(order, rem, s_head, got_p, got_s, *props)
    return force, stiff, stress, whole(new_state, 7), whole(new_props, 5)


def solution(mesh):
    in_specs = (
        P("cell", None),
        P("cell", "sec", None, None),
        P("cell", "sec", None),
        P("cell", "sec", None),
        P("cell", "sec", None),
        P("cell", "sec", None),
        P("cell", "sec", None),
        P("cell", "sec", None),
        P("cell", "sec"),
        P("cell", "sec"),
        P("cell", "sec"),
    )
    out_specs = (
        P("cell", None),
        P("cell", None),
        P("cell", "sec", None),
        P("cell", "sec", None, None),
        P("cell", "sec", None, None),
    )

    return jax.shard_map(local, mesh=mesh, in_specs=in_specs, out_specs=out_specs, check_vma=False)
```

```python
import functools
import math

import jax
import jax.numpy as jnp
import numpy as np
from jax import lax
from jax.experimental import pallas as pl
from jax.experimental.layout import Layout, with_layout_constraint
from jax.experimental.pallas import tpu as pltpu
from jax.sharding import PartitionSpec as P


GRID = 16
PLANE = GRID * GRID
LANES = 128
BATCH = 8
GAUSS = 8
SLOPE = 0.05
top_precision = lax.Precision.HIGHEST
SUMS = 29
PAIRS = 2
LINES = GRID * PLANE // LANES
P_ROWS = 5 * LINES
S_ROWS = 7 * LINES
ROWS = P_ROWS + S_ROWS
EARLY = 6


def strain_table():
    root = 1.0 / math.sqrt(3.0)
    table = np.zeros((8, 6, 24), np.float32)
    for gauss_pt in range(8):
        point = [((gauss_pt >> axis_bit & 1) * 2 - 1) * root for axis_bit in range(3)]
        for node in range(8):
            signs = [(node >> axis_bit & 1) * 2 - 1 for axis_bit in range(3)]
            grads = []
            for axis_bit in range(3):
                factor = 2.0 * signs[axis_bit] / 8.0
                for other in range(3):
                    if other != axis_bit:
                        factor = factor * (1.0 + signs[other] * point[other])
                grads.append(factor)
            table[gauss_pt, 0, 3 * node + 0] = grads[0]
            table[gauss_pt, 1, 3 * node + 1] = grads[1]
            table[gauss_pt, 2, 3 * node + 2] = grads[2]
            table[gauss_pt, 3, 3 * node + 1] = 0.5 * grads[2]
            table[gauss_pt, 3, 3 * node + 2] = 0.5 * grads[1]
            table[gauss_pt, 4, 3 * node + 0] = 0.5 * grads[2]
            table[gauss_pt, 4, 3 * node + 2] = 0.5 * grads[0]
            table[gauss_pt, 5, 3 * node + 0] = 0.5 * grads[1]
            table[gauss_pt, 5, 3 * node + 1] = 0.5 * grads[0]
    return table


def cas_tables():
    index = np.arange(GRID)
    angle = 2.0 * np.pi * (np.outer(index, index) % GRID) / GRID
    plus = np.cos(angle) + np.sin(angle)
    minus = np.cos(angle) - np.sin(angle)
    full = np.stack(
        [np.kron(plus, plus), -np.kron(minus, minus), -np.kron(plus, minus), -np.kron(minus, plus)]
    ).astype(np.float32)
    high = full.astype(jnp.bfloat16)
    low = (full - high.astype(np.float32)).astype(jnp.bfloat16)
    waves = np.sin(2.0 * np.pi * index / GRID)
    wave_y = np.repeat(waves, GRID)
    wave_z = np.tile(waves, GRID)
    squared = waves[:, None] ** 2 + wave_y[None, :] ** 2 + wave_z[None, :] ** 2
    inv_sq = np.where(squared > 0.01, 1.0 / np.maximum(squared, 0.01), 0.0)
    table = np.concatenate([inv_sq, wave_y[None], wave_z[None], np.zeros((6, PLANE))], axis=0)
    return high, low, table.astype(np.float32), [float(w) for w in waves]


def hartley(values):
    count = len(values)
    if count == 1:
        return list(values)
    half = count // 2
    even = hartley(values[0::2])
    odd = hartley(values[1::2])
    low, high = [], []
    for k in range(half):
        other = odd[(-k) % half]
        if k == 0:
            term = odd[0]
        elif 4 * k == count:
            term = other
        elif 8 * k == count:
            term = (odd[k] + other) * math.sqrt(0.5)
        elif 8 * k == 3 * count:
            term = (other - odd[k]) * math.sqrt(0.5)
        else:
            turn = 2.0 * math.pi * k / count
            term = odd[k] * math.cos(turn) + other * math.sin(turn)
        low.append(even[k] + term)
        high.append(even[k] - term)
    return low + high


def pack_kernel(elems, points, first, flag, *refs):
    *sources, order, head = refs
    total = elems * points

    def place(wanted, start):
        def step(cell, at):
            hit = (flag[cell // points, cell % points] > 0) == wanted

            @pl.when(hit)
            def _():
                order[at] = cell
                order[total + 1 + cell] = at

            return at + hit.astype(jnp.int32)

        return lax.fori_loop(0, total, step, start)

    moving = place(True, jnp.int32(0))
    place(False, moving)
    order[total] = moving

    for slot in range(first):
        cell = order[slot]
        at = (cell // points) * (LINES * points) + cell % points
        for row, source in enumerate(sources):
            for part in range(0, LINES, 8):
                head[slot, row * LINES + part : row * LINES + part + 8, :] = source[
                    pl.ds(at + part * points, 8, stride=points), :
                ]


def solve_kernel(
    elems,
    points,
    begin,
    first,
    waves,
    order,
    fft_iters,
    rm_iters,
    disp,
    bmat,
    plastic,
    hard,
    shear,
    bulk,
    base,
    sat,
    rate,
    high,
    low,
    table,
    other,
    after,
    sums,
    rec,
    field,
    work,
    spec,
    parts,
    acc,
):
    total = elems * points
    block = GRID * BATCH
    row_of = lax.broadcasted_iota(jnp.int32, (BATCH, LANES), 0)

    cells = [order[min(begin + slot, total - 1)] for slot in range(BATCH)]

    section = lax.axis_index("sec")

    def fill(slot, carry):
        cell = order[jnp.minimum(begin + slot, total - 1)]
        e_at, g_at = cell // points, cell % points
        for half in range(2):
            for part in range(2):
                near = (part * 16 + half) * points + g_at
                here = part * 64 + slot
                for comp in range(6):
                    at = (e_at * 6 + comp) * (LINES * points) + near
                    rec[half, pl.ds(comp * block + here, 8, stride=BATCH), :] = plastic[
                        pl.ds(at, 8, stride=2 * points), :
                    ]
                for row, source in enumerate((hard, shear, bulk, base, sat, rate)):
                    at = e_at * (LINES * points) + near
                    rec[half, pl.ds((6 + row) * block + here, 8, stride=BATCH), :] = source[
                        pl.ds(at, 8, stride=2 * points), :
                    ]
        value = jnp.sum(bmat[section * points + g_at] * disp[e_at], axis=1, keepdims=True)
        acc[pl.ds(0, 6), pl.ds(slot, 1), :] = jnp.broadcast_to(value, (6, LANES))[:, None, :]
        return carry

    lax.fori_loop(0, BATCH, fill, 0)

    def per_cell(pick, dtype):
        out = jnp.zeros((BATCH, LANES), dtype)
        for slot in range(BATCH):
            out = jnp.where(row_of == slot, pick(slot), out)
        return out

    fft_count = per_cell(lambda s: fft_iters[cells[s] // points, cells[s] % points], jnp.int32)
    rm_count = per_cell(lambda s: rm_iters[cells[s] // points, cells[s] % points], jnp.int32)
    most = functools.reduce(
        jnp.maximum, [fft_iters[c // points, c % points] for c in cells]
    )

    def extremes(row):
        top = bottom = None
        for half in range(2):
            for x in range(GRID):
                value = rec[half, row * block + x * BATCH : row * block + (x + 1) * BATCH, :]
                top = value if top is None else jnp.maximum(top, value)
                bottom = value if bottom is None else jnp.minimum(bottom, value)
        return 0.5 * (
            jnp.max(top, axis=1, keepdims=True) + jnp.min(bottom, axis=1, keepdims=True)
        )

    mu_ref = extremes(7)
    bulk_ref = extremes(8)
    lame_ref = bulk_ref - 2.0 * mu_ref / 3.0
    coupling = jnp.broadcast_to((lame_ref + mu_ref) / (lame_ref + 2.0 * mu_ref), (BATCH, LANES))
    inv_mu = jnp.broadcast_to(1.0 / (mu_ref * (GRID * PLANE)), (BATCH, LANES))

    for comp in range(6):
        value = jnp.concatenate([acc[comp]] * 2, axis=0)

        def start(pair, carry):
            for half in range(2):
                field[half, pl.ds(comp * block + pair * 16, 16), :] = value
            return carry

        lax.fori_loop(0, GRID // 2, start, 0)

    def prepare(pair, carry):
        for half in range(2):
            load = lambda row: rec[half, pl.ds(row * block + pair * 16, 16), :]
            level, mu, sat, rate = load(6), load(7), load(10), load(11)
            decay = jnp.exp(-rate * level)
            rec[half, pl.ds(12 * block + pair * 16, 16), :] = (
                load(9) + sat * (1.0 - decay) + SLOPE * level
            )
            rest = sat * decay
            rec[half, pl.ds(13 * block + pair * 16, 16), :] = rest
            rec[half, pl.ds(14 * block + pair * 16, 16), :] = 1.0 / (
                3.0 * mu + rest * rate + SLOPE
            )
        return carry

    lax.fori_loop(0, GRID // 2, prepare, 0)

    rm_pair = jnp.concatenate([rm_count] * 2, axis=0)
    second, third = rm_pair > 1, rm_pair > 2

    def newton(over, inc, mu3, rest, rate):
        decay = jnp.exp(-rate * inc)
        num = over - mu3 * inc - rest * (1.0 - decay)
        return inc + num / (mu3 + rest * rate * decay)

    def trial(half, pair):
        load = lambda row: rec[half, pl.ds(row * block + pair * 16, 16), :]
        elastic = [
            field[half, pl.ds(comp * block + pair * 16, 16), :] - load(comp) for comp in range(6)
        ]
        volume = elastic[0] + elastic[1] + elastic[2]
        mu = load(7)
        mu2 = 2.0 * mu
        mean = volume * (1.0 / 3.0)
        dev = [mu2 * (part - mean) for part in elastic[:3]] + [mu2 * part for part in elastic[3:]]
        squared = 1.5 * (dev[0] * dev[0] + dev[1] * dev[1] + dev[2] * dev[2]) + 3.0 * (
            dev[3] * dev[3] + dev[4] * dev[4] + dev[5] * dev[5]
        )
        return load, volume, mu, dev, squared

    def increments(load, mu, over):
        mu3 = 3.0 * mu + SLOPE
        rest, rate = load(13), load(11)
        inc = over * load(14)
        inc = jnp.where(second, newton(over, inc, mu3, rest, rate), inc)
        return jnp.where(third, newton(over, inc, mu3, rest, rate), inc)

    def split_rows(comp):
        if comp < 3:
            return comp * block, (3 + comp) * block
        return 2 * comp * block, (2 * comp + 1) * block

    def split_store(comp, pair, half, value):
        upper = value.astype(jnp.bfloat16)
        lower = (value - upper.astype(jnp.float32)).astype(jnp.bfloat16)
        lanes = slice(half * LANES, (half + 1) * LANES)
        for base, part in zip(split_rows(comp), (upper, lower)):
            parts[pl.ds(base + pair * 16, 16), lanes] = part

    def stress_pair(pair):
        for half in range(2):
            load, volume, mu, dev, squared = trial(half, pair)
            base = load(9)
            capped = jnp.maximum(squared, base * base)
            inv_eq = lax.rsqrt(capped)
            over = jnp.maximum(capped * inv_eq - load(12), 0.0)
            inc = increments(load, mu, over)
            shrink = 1.0 - 3.0 * mu * inc * inv_eq
            pressure = load(8) * volume
            for comp in range(6):
                value = shrink * dev[comp]
                if comp < 3:
                    value = value + pressure
                split_store(comp, pair, half, value)

    def stress_step(step, carry):
        for near in range(PAIRS):
            stress_pair(step * PAIRS + near)
        return carry

    def plane_product(store):
        dot = functools.partial(jnp.dot, preferred_element_type=jnp.float32)
        for which, comps in enumerate(((0, 1, 2), (3,), (4,), (5,))):
            from_row, rows = split_rows(comps[0])[0], len(comps) * block
            both = dot(parts[from_row : from_row + 2 * rows, :], high[which])
            rest = dot(parts[from_row : from_row + rows, :], low[which])
            store(comps[0] * block, both[:rows] + (both[rows:] + rest))

    def store_spec(at, value):
        for half in range(2):
            work[half, at : at + value.shape[0], :] = value[:, half * LANES : (half + 1) * LANES]

    def update_field(at, value):
        for half in range(2):
            field[half, at : at + value.shape[0], :] = (
                field[half, at : at + value.shape[0], :]
                - value[:, half * LANES : (half + 1) * LANES]
            )

    def flip(comp, k):
        return (-k) % GRID if comp in (4, 5) else k

    def sweep(index, carry):
        lax.fori_loop(0, GRID // (2 * PAIRS), stress_step, 0)
        plane_product(store_spec)
        scale_cell = jnp.where(index < fft_count, inv_mu, 0.0)

        def spectral(half, inner):
            for comp in range(6):
                lines = hartley(
                    [
                        work[half, comp * block + x * BATCH : comp * block + (x + 1) * BATCH, :]
                        for x in range(GRID)
                    ]
                )
                for k in range(GRID):
                    at = comp * block + flip(comp, k) * BATCH
                    spec[half, at : at + BATCH, :] = lines[k]
            wave_y = jnp.broadcast_to(table[half, GRID : GRID + 1, :], (BATCH, LANES))
            wave_z = jnp.broadcast_to(table[half, GRID + 1 : GRID + 2, :], (BATCH, LANES))
            for k in range(GRID):
                wave_x = waves[k]
                inv_sq = jnp.broadcast_to(table[half, k : k + 1, :], (BATCH, LANES))
                s = [
                    spec[half, comp * block + k * BATCH : comp * block + (k + 1) * BATCH, :]
                    for comp in range(6)
                ]
                comp_a = s[0] * wave_x + s[5] * wave_y + s[4] * wave_z
                comp_b = s[5] * wave_x + s[1] * wave_y + s[3] * wave_z
                comp_c = s[4] * wave_x + s[3] * wave_y + s[2] * wave_z
                along = (wave_x * comp_a + wave_y * comp_b + wave_z * comp_c) * (
                    inv_sq * coupling
                )
                scale = inv_sq * scale_cell
                vec_a = (comp_a - along * wave_x) * scale
                vec_b = (comp_b - along * wave_y) * scale
                vec_c = (comp_c - along * wave_z) * scale
                mapped = (
                    wave_x * vec_a,
                    wave_y * vec_b,
                    wave_z * vec_c,
                    0.5 * (wave_y * vec_c + wave_z * vec_b),
                    0.5 * (wave_x * vec_c + wave_z * vec_a),
                    0.5 * (wave_x * vec_b + wave_y * vec_a),
                )
                for comp in range(6):
                    at = comp * block + flip(comp, k) * BATCH
                    work[half, at : at + BATCH, :] = mapped[comp]
            return inner

        for half in range(2):
            spectral(half, 0)
            for comp in range(6):
                lines = hartley(
                    [
                        work[half, comp * block + x * BATCH : comp * block + (x + 1) * BATCH, :]
                        for x in range(GRID)
                    ]
                )
                for pair in range(GRID // 2):
                    value = jnp.concatenate([lines[2 * pair], lines[2 * pair + 1]], axis=0)
                    split_store(comp, pair, half, value)
        plane_product(update_field)
        return carry

    lax.fori_loop(0, most, sweep, 0)

    acc[...] = jnp.zeros_like(acc)

    def finish(pair, carry):
        for half in range(2):
            load, volume, mu, dev, squared = trial(half, pair)
            base = load(9)
            trial_eq = jnp.sqrt(squared)
            excess = trial_eq - load(12)
            over = jnp.maximum(excess, 0.0)
            inc = increments(load, mu, over)
            inv_eq = 1.0 / jnp.maximum(trial_eq, base)
            lost = 3.0 * mu * inc * inv_eq
            shrink = 1.0 - lost
            pressure = load(8) * volume
            grow = 1.5 * inc * inv_eq
            for comp in range(6):
                work[half, pl.ds(comp * block + pair * 16, 16), :] = load(comp) + grow * dev[comp]
            spec[half, pl.ds(pair * 16, 16), :] = load(6) + inc
            rate = load(11)
            slope = load(13) * rate * jnp.exp(-rate * inc) + SLOPE
            corr = jnp.where(excess > 0.0, 3.0 * mu / (3.0 * mu + slope) - lost, 0.0)
            weight = 3.0 * mu * corr * (inv_eq * inv_eq)
            terms = [shrink * part for part in dev]
            terms = [term + pressure for term in terms[:3]] + terms[3:]
            terms.append(load(8))
            terms.append(2.0 * mu * shrink)
            for c in range(6):
                scaled = weight * dev[c]
                for d in range(c, 6):
                    terms.append(scaled * dev[d])
            for at, term in enumerate(terms):
                acc[at] = acc[at] + (term[:BATCH] + term[BATCH:])
        return carry

    lax.fori_loop(0, GRID // 2, finish, 0)

    lane_of = lax.broadcasted_iota(jnp.int32, (BATCH, LANES), 1)
    out = jnp.zeros((BATCH, LANES), jnp.float32)
    for at in range(SUMS):
        out = jnp.where(lane_of == at, jnp.sum(acc[at], axis=1, keepdims=True), out)
    sums[...] = out * (1.0 / (GRID * PLANE))

    ahead = max(begin - first, 0)
    if begin:
        for at in range(ahead):
            after[at] = other[at]
    for slot in range(min(BATCH, total - begin)):
        alone = begin == 0 and slot < first
        target = other if alone else after
        here = slot if alone else begin + slot - first
        for half in range(2):
            for part in range(2):
                near = part * 16 + half
                for row in range(7):
                    source, from_row = (work, row) if row < 6 else (spec, 0)
                    at = (0 if alone else P_ROWS) + row * LINES + near
                    target[here, pl.ds(at, 8, stride=2), :] = source[
                        half, pl.ds(from_row * block + part * 64 + slot, 8, stride=BATCH), :
                    ]
                if not alone:
                    for row in range(5):
                        target[here, pl.ds(row * LINES + near, 8, stride=2), :] = rec[
                            half, pl.ds((7 + row) * block + part * 64 + slot, 8, stride=BATCH), :
                        ]


def put_cell(target, cell, points, count, load):
    for row in range(count):
        for part in range(0, LINES, 8):
            at = (row * LINES + part) * points + cell % points
            target[cell // points, pl.ds(at, 8, stride=points), :] = load(row * LINES + part)


def gather_kernel(
    elems,
    points,
    first,
    order,
    rem,
    s_head,
    got_p,
    got_s,
    shear,
    bulk,
    base,
    sat,
    rate,
    s_out,
    p_out,
    cells,
    in_sem,
):
    total = elems * points
    moving = order[total]
    rows = LINES * points

    def arrival(slot):
        late = slot - first
        return pltpu.make_async_copy(rem.at[late], cells.at[late], in_sem.at[late])

    from_slot = jnp.maximum(moving, first)

    @pl.loop(from_slot, total)
    def _(slot):
        arrival(slot).start()

    @pl.loop(0, elems)
    def _(e_at):
        for row, source in enumerate((shear, bulk, base, sat, rate)):
            p_out[e_at, pl.ds(row * rows, rows), :] = source[
                pl.ds(pl.multiple_of(e_at * rows, rows), rows), :
            ]

    @pl.loop(0, first)
    def _(slot):
        cell = order[slot]

        @pl.when(slot < moving)
        def _():
            put_cell(p_out, cell, points, 5, lambda at: got_p[slot, at : at + 8, :])
            put_cell(s_out, cell, points, 7, lambda at: got_s[slot, at : at + 8, :])

        @pl.when(slot >= moving)
        def _():
            put_cell(s_out, cell, points, 7, lambda at: s_head[slot, at : at + 8, :])

    @pl.loop(from_slot, total)
    def _(slot):
        late = slot - first
        arrival(slot).wait()
        put_cell(
            s_out,
            order[slot],
            points,
            7,
            lambda at: cells[late, P_ROWS + at : P_ROWS + at + 8, :],
        )


def finish_kernel(
    elems, points, first, count, order, near_s, near_p, *refs
):
    got = refs[0] if count else None
    new_state, new_props, s_out, p_out, out_sem = refs[1 if count else 0 :]
    total = elems * points

    def leaving(e_at):
        return (
            pltpu.make_async_copy(s_out.at[e_at], new_state.at[e_at], out_sem.at[e_at, 0]),
            pltpu.make_async_copy(p_out.at[e_at], new_props.at[e_at], out_sem.at[e_at, 1]),
        )

    @pl.loop(0, elems)
    def _(e_at):
        s_out[e_at] = near_s[e_at]
        p_out[e_at] = near_p[e_at]
        if count:

            @pl.loop(0, points)
            def _(g_at):
                cell = e_at * points + g_at
                slot = order[total + 1 + cell]
                late = jnp.clip(slot - first, 0, count - 1)

                @pl.when((slot >= first) & (slot < first + count))
                def _():
                    put_cell(p_out, cell, points, 5, lambda at: got[late, at : at + 8, :])
                    put_cell(
                        s_out,
                        cell,
                        points,
                        7,
                        lambda at: got[late, P_ROWS + at : P_ROWS + at + 8, :],
                    )

        for copy in leaving(e_at):
            copy.start()

    @pl.loop(0, elems)
    def _(e_at):
        for copy in leaving(e_at):
            copy.wait()


def element_terms(table_part, sums, points):
    elems = sums.shape[0] // points
    weights = np.array([1.0, 1.0, 1.0, 2.0, 2.0, 2.0], np.float32)
    stress = sums[:, 0:6]
    block = np.outer([1.0, 1.0, 1.0, 0.0, 0.0, 0.0], [1.0, 1.0, 1.0, 0.0, 0.0, 0.0])
    spread = np.zeros((23, 36), np.float32)
    spread[0] = block.reshape(36)
    spread[1] = (np.eye(6) - block / 3.0).reshape(36)
    at = 2
    for c in range(6):
        for d in range(c, 6):
            spread[at, 6 * c + d] = -weights[d]
            spread[at, 6 * d + c] = -weights[c]
            at += 1
    tangent = jnp.dot(sums[:, 6:SUMS], spread, precision=top_precision)
    stress_part = stress.reshape(elems, points, 6)
    force = (
        jnp.einsum("egc,gcn->en", stress_part * weights, table_part, precision=top_precision)
        / GAUSS
    )
    scaled = tangent.reshape(elems, points, 6, 6) * weights[None, None, :, None]
    stiff = (
        jnp.einsum(
            "gcn,egcd,gdm->enm", table_part, scaled, table_part, precision=top_precision
        ).reshape(elems, 576)
        / GAUSS
    )
    return stress_part, force, stiff


VMEM = pl.BlockSpec(memory_space=pltpu.VMEM)
SMEM = pl.BlockSpec(memory_space=pltpu.SMEM)
ANY = pl.BlockSpec(memory_space=pl.ANY)
GRANT = 60 * 2**20
MERGE_GRANT = 24 * 2**20


def shape(*dims, dtype=jnp.float32):
    return jax.ShapeDtypeStruct(dims, dtype)


def local(
    elem_disp,
    plastic_strain,
    hardening_var,
    shear_mod,
    bulk_mod,
    yield_stress,
    sat_stress,
    sat_rate,
    fft_iters,
    rm_iters,
    move_flag,
):
    elems, points = plastic_strain.shape[:2]
    voxels = plastic_strain.shape[3]
    total = elems * points
    group = min(BATCH, total)
    first = max(1, total * EARLY // 16)
    devices = lax.axis_size("cell")
    route = [((i - devices // 2) % devices, i) for i in range(devices)]

    params = pltpu.CompilerParams(vmem_limit_bytes=GRANT)
    bmat = jnp.asarray(strain_table())

    def flat(array):
        lead = array.shape[2:-1]
        tiles = array.reshape(elems, points, *lead, LINES, LANES)
        return jnp.moveaxis(tiles, 1, -2).reshape(-1, LANES)

    def whole(lines, lead):
        tiles = lines.reshape(elems, lead, LINES, points, LANES)
        tiles = with_layout_constraint(jnp.moveaxis(tiles, 3, 1), Layout((0, 2, 3, 1, 4)))
        return tiles.reshape(elems, points, lead, voxels)

    props = [flat(a) for a in (shear_mod, bulk_mod, yield_stress, sat_stress, sat_rate)]
    hard, plastic = flat(hardening_var), flat(plastic_strain)
    order, p_head = pl.pallas_call(
        functools.partial(pack_kernel, elems, points, first),
        out_shape=(shape(2 * total + 1, dtype=jnp.int32), shape(first, P_ROWS, LANES)),
        in_specs=[SMEM] + [VMEM] * 5,
        out_specs=(SMEM, VMEM),
        compiler_params=params,
        name="pack",
    )(move_flag, *props)

    got_p = lax.ppermute(p_head, "cell", route)

    high, low, table, waves = cas_tables()
    table = table.reshape(24, 2, LANES).transpose(1, 0, 2)
    block = GRID * BATCH
    disp = elem_disp.reshape(elems, 1, elem_disp.shape[1])

    def solve(begin, count, other=None):
        late = shape(count, ROWS, LANES)
        alone = () if begin else (shape(first, S_ROWS, LANES),)
        return pl.pallas_call(
            functools.partial(solve_kernel, elems, points, begin, first, waves),
            out_shape=alone + (late, shape(BATCH, LANES)),
            in_specs=[SMEM] * 3 + [VMEM] * (13 if begin else 12),
            out_specs=(VMEM,) * (len(alone) + 2),
            scratch_shapes=[
                pltpu.VMEM((2, 15 * block, LANES), jnp.float32),
                pltpu.VMEM((2, 6 * block, LANES), jnp.float32),
                pltpu.VMEM((2, 6 * block, LANES), jnp.float32),
                pltpu.VMEM((2, 6 * block, LANES), jnp.float32),
                pltpu.VMEM((2 * 6 * block, PLANE), jnp.bfloat16),
                pltpu.VMEM((SUMS, BATCH, LANES), jnp.float32),
            ],
            compiler_params=params,
            cost_estimate=pl.CostEstimate(
                flops=20 * 10**9, bytes_accessed=8 * 10**6, transcendentals=0
            ),
            name="solve",
        )(
            order,
            fft_iters,
            rm_iters,
            disp,
            bmat,
            plastic,
            hard,
            *props,
            high,
            low,
            table,
            *(() if other is None else (other,)),
        )

    s_head, rem, sums = solve(0, group - first)
    got_s = lax.ppermute(s_head, "cell", route)
    if total > group:
        rem, more = solve(group, total - first, rem)
        sums = jnp.concatenate([sums, more], axis=0)

    slots = order[:total]
    place = (slots[None, :] == jnp.arange(total)[:, None]).astype(jnp.float32)
    sums = jnp.dot(place, sums[:total], precision=top_precision)
    table_part = lax.dynamic_slice_in_dim(bmat, lax.axis_index("sec") * points, points, 0)
    stress, force_part, stiff_part = element_terms(table_part, sums, points)
    sections = lax.axis_size("sec")
    force, stiff = force_part, stiff_part
    for step in range(1, sections):
        ring = [((i - step) % sections, i) for i in range(sections)]
        force = force + lax.ppermute(force_part, "sec", ring)
        stiff = stiff + lax.ppermute(stiff_part, "sec", ring)
    rem, force, stiff, stress = lax.optimization_barrier((rem, force, stiff, stress))

    blocks = (
        shape(elems, 7 * LINES * points, LANES),
        shape(elems, 5 * LINES * points, LANES),
    )
    ends = pltpu.CompilerParams(vmem_limit_bytes=MERGE_GRANT)

    def branch(count):
        def run(order, rem, s_head, got_p, got_s, *props):
            late = ()
            if count:
                late = (lax.ppermute(rem[:count], "cell", route),)
            near = pl.pallas_call(
                functools.partial(gather_kernel, elems, points, first),
                out_shape=blocks,
                in_specs=[SMEM, ANY] + [VMEM] * 8,
                out_specs=(VMEM, VMEM),
                scratch_shapes=[
                    pltpu.VMEM((total - first, ROWS, LANES), jnp.float32),
                    pltpu.SemaphoreType.DMA((total - first,)),
                ],
                compiler_params=ends,
                cost_estimate=pl.CostEstimate(
                    flops=10**9, bytes_accessed=6 * 10**6, transcendentals=0
                ),
                name="gather",
            )(order, rem, s_head, got_p, got_s, *props)
            new_state, new_props = pl.pallas_call(
                functools.partial(finish_kernel, elems, points, first, count),
                out_shape=blocks,
                in_specs=[SMEM] + [VMEM] * (2 + len(late)),
                out_specs=(ANY, ANY),
                scratch_shapes=[
                    *[pltpu.VMEM(block.shape, jnp.float32) for block in blocks],
                    pltpu.SemaphoreType.DMA((elems, 2)),
                ],
                compiler_params=ends,
                name="finish",
            )(order, *near, *late)
            return new_state, new_props

        return run

    extra = jnp.clip(
        jnp.sum((move_flag > 0).astype(jnp.int32)) - first, 0, total - first
    )
    new_state, new_props = lax.switch(
        extra,
        [branch(c) for c in range(total - first + 1)],
        order,
        rem,
        s_head,
        got_p,
        got_s,
        *props,
    )
    return force, stiff, stress, whole(new_state, 7), whole(new_props, 5)


def solution(mesh):
    in_specs = (
        P("cell", None),
        P("cell", "sec", None, None),
        P("cell", "sec", None),
        P("cell", "sec", None),
        P("cell", "sec", None),
        P("cell", "sec", None),
        P("cell", "sec", None),
        P("cell", "sec", None),
        P("cell", "sec"),
        P("cell", "sec"),
        P("cell", "sec"),
    )
    out_specs = (
        P("cell", None),
        P("cell", None),
        P("cell", "sec", None),
        P("cell", "sec", None, None),
        P("cell", "sec", None, None),
    )

    return jax.shard_map(local, mesh=mesh, in_specs=in_specs, out_specs=out_specs, check_vma=False)
```

```python
import functools
import math

import jax
import jax.numpy as jnp
import numpy as np
from jax import lax
from jax.experimental import pallas as pl
from jax.experimental.pallas import tpu as pltpu
from jax.sharding import PartitionSpec as P


GRID = 16
PLANE = GRID * GRID
LANES = 128
BATCH = 8
GAUSS = 8
SLOPE = 0.05
top_precision = lax.Precision.HIGHEST
SUMS = 29
PAIRS = 2
LINES = GRID * PLANE // LANES
P_ROWS = 5 * LINES
S_ROWS = 7 * LINES
ROWS = P_ROWS + S_ROWS
EARLY = 7


def strain_table():
    root = 1.0 / math.sqrt(3.0)
    table = np.zeros((8, 6, 24), np.float32)
    for gauss_pt in range(8):
        point = [((gauss_pt >> axis_bit & 1) * 2 - 1) * root for axis_bit in range(3)]
        for node in range(8):
            signs = [(node >> axis_bit & 1) * 2 - 1 for axis_bit in range(3)]
            grads = []
            for axis_bit in range(3):
                factor = 2.0 * signs[axis_bit] / 8.0
                for other in range(3):
                    if other != axis_bit:
                        factor = factor * (1.0 + signs[other] * point[other])
                grads.append(factor)
            table[gauss_pt, 0, 3 * node + 0] = grads[0]
            table[gauss_pt, 1, 3 * node + 1] = grads[1]
            table[gauss_pt, 2, 3 * node + 2] = grads[2]
            table[gauss_pt, 3, 3 * node + 1] = 0.5 * grads[2]
            table[gauss_pt, 3, 3 * node + 2] = 0.5 * grads[1]
            table[gauss_pt, 4, 3 * node + 0] = 0.5 * grads[2]
            table[gauss_pt, 4, 3 * node + 2] = 0.5 * grads[0]
            table[gauss_pt, 5, 3 * node + 0] = 0.5 * grads[1]
            table[gauss_pt, 5, 3 * node + 1] = 0.5 * grads[0]
    return table


def cas_tables():
    index = np.arange(GRID)
    angle = 2.0 * np.pi * (np.outer(index, index) % GRID) / GRID
    plus = np.cos(angle) + np.sin(angle)
    minus = np.cos(angle) - np.sin(angle)
    full = np.stack(
        [np.kron(plus, plus), -np.kron(minus, minus), -np.kron(plus, minus), -np.kron(minus, plus)]
    ).astype(np.float32)
    high = full.astype(jnp.bfloat16)
    low = (full - high.astype(np.float32)).astype(jnp.bfloat16)
    waves = np.sin(2.0 * np.pi * index / GRID)
    wave_y = np.repeat(waves, GRID)
    wave_z = np.tile(waves, GRID)
    squared = waves[:, None] ** 2 + wave_y[None, :] ** 2 + wave_z[None, :] ** 2
    inv_sq = np.where(squared > 0.01, 1.0 / np.maximum(squared, 0.01), 0.0)
    table = np.concatenate([inv_sq, wave_y[None], wave_z[None], np.zeros((6, PLANE))], axis=0)
    return high, low, table.astype(np.float32), [float(w) for w in waves]


def hartley(values):
    count = len(values)
    if count == 1:
        return list(values)
    half = count // 2
    even = hartley(values[0::2])
    odd = hartley(values[1::2])
    low, high = [], []
    for k in range(half):
        other = odd[(-k) % half]
        if k == 0:
            term = odd[0]
        elif 4 * k == count:
            term = other
        elif 8 * k == count:
            term = (odd[k] + other) * math.sqrt(0.5)
        elif 8 * k == 3 * count:
            term = (other - odd[k]) * math.sqrt(0.5)
        else:
            turn = 2.0 * math.pi * k / count
            term = odd[k] * math.cos(turn) + other * math.sin(turn)
        low.append(even[k] + term)
        high.append(even[k] - term)
    return low + high


def pack_kernel(elems, points, first, flag, *refs):
    *sources, order, head = refs
    total = elems * points

    def place(wanted, start):
        def step(cell, at):
            hit = (flag[cell // points, cell % points] > 0) == wanted

            @pl.when(hit)
            def _():
                order[at] = cell
                order[total + 1 + cell] = at

            return at + hit.astype(jnp.int32)

        return lax.fori_loop(0, total, step, start)

    moving = place(True, jnp.int32(0))
    place(False, moving)
    order[total] = moving

    for slot in range(first):
        cell = order[slot]
        at = (cell // points) * (LINES * points) + cell % points
        for row, source in enumerate(sources):
            for part in range(0, LINES, 8):
                head[slot, row * LINES + part : row * LINES + part + 8, :] = source[
                    pl.ds(at + part * points, 8, stride=points), :
                ]


def solve_kernel(
    elems,
    points,
    begin,
    first,
    waves,
    order,
    fft_iters,
    rm_iters,
    disp,
    bmat,
    plastic,
    hard,
    shear,
    bulk,
    base,
    sat,
    rate,
    high,
    low,
    table,
    other,
    after,
    sums,
    rec,
    field,
    work,
    spec,
    parts,
    acc,
):
    total = elems * points
    block = GRID * BATCH
    row_of = lax.broadcasted_iota(jnp.int32, (BATCH, LANES), 0)

    cells = [order[min(begin + slot, total - 1)] for slot in range(BATCH)]

    section = lax.axis_index("sec")

    def fill(slot, carry):
        cell = order[jnp.minimum(begin + slot, total - 1)]
        e_at, g_at = cell // points, cell % points
        for half in range(2):
            for part in range(2):
                near = (part * 16 + half) * points + g_at
                here = part * 64 + slot
                for comp in range(6):
                    at = (e_at * 6 + comp) * (LINES * points) + near
                    rec[half, pl.ds(comp * block + here, 8, stride=BATCH), :] = plastic[
                        pl.ds(at, 8, stride=2 * points), :
                    ]
                for row, source in enumerate((hard, shear, bulk, base, sat, rate)):
                    at = e_at * (LINES * points) + near
                    rec[half, pl.ds((6 + row) * block + here, 8, stride=BATCH), :] = source[
                        pl.ds(at, 8, stride=2 * points), :
                    ]
        value = jnp.sum(bmat[section * points + g_at] * disp[e_at], axis=1, keepdims=True)
        acc[pl.ds(0, 6), pl.ds(slot, 1), :] = jnp.broadcast_to(value, (6, LANES))[:, None, :]
        return carry

    lax.fori_loop(0, BATCH, fill, 0)

    def per_cell(pick, dtype):
        out = jnp.zeros((BATCH, LANES), dtype)
        for slot in range(BATCH):
            out = jnp.where(row_of == slot, pick(slot), out)
        return out

    fft_count = per_cell(lambda s: fft_iters[cells[s] // points, cells[s] % points], jnp.int32)
    rm_count = per_cell(lambda s: rm_iters[cells[s] // points, cells[s] % points], jnp.int32)
    most = functools.reduce(
        jnp.maximum, [fft_iters[c // points, c % points] for c in cells]
    )

    def extremes(row):
        top = bottom = None
        for half in range(2):
            for x in range(GRID):
                value = rec[half, row * block + x * BATCH : row * block + (x + 1) * BATCH, :]
                top = value if top is None else jnp.maximum(top, value)
                bottom = value if bottom is None else jnp.minimum(bottom, value)
        return 0.5 * (
            jnp.max(top, axis=1, keepdims=True) + jnp.min(bottom, axis=1, keepdims=True)
        )

    mu_ref = extremes(7)
    bulk_ref = extremes(8)
    lame_ref = bulk_ref - 2.0 * mu_ref / 3.0
    coupling = jnp.broadcast_to((lame_ref + mu_ref) / (lame_ref + 2.0 * mu_ref), (BATCH, LANES))
    inv_mu = jnp.broadcast_to(1.0 / (mu_ref * (GRID * PLANE)), (BATCH, LANES))

    for comp in range(6):
        value = jnp.concatenate([acc[comp]] * 2, axis=0)

        def start(pair, carry):
            for half in range(2):
                field[half, pl.ds(comp * block + pair * 16, 16), :] = value
            return carry

        lax.fori_loop(0, GRID // 2, start, 0)

    def prepare(pair, carry):
        for half in range(2):
            load = lambda row: rec[half, pl.ds(row * block + pair * 16, 16), :]
            level, mu, sat, rate = load(6), load(7), load(10), load(11)
            decay = jnp.exp(-rate * level)
            rec[half, pl.ds(12 * block + pair * 16, 16), :] = (
                load(9) + sat * (1.0 - decay) + SLOPE * level
            )
            rest = sat * decay
            rec[half, pl.ds(13 * block + pair * 16, 16), :] = rest
            rec[half, pl.ds(14 * block + pair * 16, 16), :] = 1.0 / (
                3.0 * mu + rest * rate + SLOPE
            )
        return carry

    lax.fori_loop(0, GRID // 2, prepare, 0)

    rm_pair = jnp.concatenate([rm_count] * 2, axis=0)
    second, third = rm_pair > 1, rm_pair > 2

    def newton(over, inc, mu3, rest, rate):
        decay = jnp.exp(-rate * inc)
        num = over - mu3 * inc - rest * (1.0 - decay)
        return inc + num / (mu3 + rest * rate * decay)

    def trial(half, pair):
        load = lambda row: rec[half, pl.ds(row * block + pair * 16, 16), :]
        elastic = [
            field[half, pl.ds(comp * block + pair * 16, 16), :] - load(comp) for comp in range(6)
        ]
        volume = elastic[0] + elastic[1] + elastic[2]
        mu = load(7)
        mu2 = 2.0 * mu
        mean = volume * (1.0 / 3.0)
        dev = [mu2 * (part - mean) for part in elastic[:3]] + [mu2 * part for part in elastic[3:]]
        squared = 1.5 * (dev[0] * dev[0] + dev[1] * dev[1] + dev[2] * dev[2]) + 3.0 * (
            dev[3] * dev[3] + dev[4] * dev[4] + dev[5] * dev[5]
        )
        return load, volume, mu, dev, squared

    def increments(load, mu, over):
        mu3 = 3.0 * mu + SLOPE
        rest, rate = load(13), load(11)
        inc = over * load(14)
        inc = jnp.where(second, newton(over, inc, mu3, rest, rate), inc)
        return jnp.where(third, newton(over, inc, mu3, rest, rate), inc)

    def split_rows(comp):
        if comp < 3:
            return comp * block, (3 + comp) * block
        return 2 * comp * block, (2 * comp + 1) * block

    def split_store(comp, pair, half, value):
        upper = value.astype(jnp.bfloat16)
        lower = (value - upper.astype(jnp.float32)).astype(jnp.bfloat16)
        lanes = slice(half * LANES, (half + 1) * LANES)
        for base, part in zip(split_rows(comp), (upper, lower)):
            parts[pl.ds(base + pair * 16, 16), lanes] = part

    def stress_pair(pair):
        for half in range(2):
            load, volume, mu, dev, squared = trial(half, pair)
            base = load(9)
            capped = jnp.maximum(squared, base * base)
            inv_eq = lax.rsqrt(capped)
            over = jnp.maximum(capped * inv_eq - load(12), 0.0)
            inc = increments(load, mu, over)
            shrink = 1.0 - 3.0 * mu * inc * inv_eq
            pressure = load(8) * volume
            for comp in range(6):
                value = shrink * dev[comp]
                if comp < 3:
                    value = value + pressure
                split_store(comp, pair, half, value)

    def stress_step(step, carry):
        for near in range(PAIRS):
            stress_pair(step * PAIRS + near)
        return carry

    def plane_product(store):
        dot = functools.partial(jnp.dot, preferred_element_type=jnp.float32)
        for which, comps in enumerate(((0, 1, 2), (3,), (4,), (5,))):
            from_row, rows = split_rows(comps[0])[0], len(comps) * block
            both = dot(parts[from_row : from_row + 2 * rows, :], high[which])
            rest = dot(parts[from_row : from_row + rows, :], low[which])
            store(comps[0] * block, both[:rows] + (both[rows:] + rest))

    def store_spec(at, value):
        for half in range(2):
            work[half, at : at + value.shape[0], :] = value[:, half * LANES : (half + 1) * LANES]

    def update_field(at, value):
        for half in range(2):
            field[half, at : at + value.shape[0], :] = (
                field[half, at : at + value.shape[0], :]
                - value[:, half * LANES : (half + 1) * LANES]
            )

    def flip(comp, k):
        return (-k) % GRID if comp in (4, 5) else k

    def sweep(index, carry):
        lax.fori_loop(0, GRID // (2 * PAIRS), stress_step, 0)
        plane_product(store_spec)
        scale_cell = jnp.where(index < fft_count, inv_mu, 0.0)

        def spectral(half, inner):
            for comp in range(6):
                lines = hartley(
                    [
                        work[half, comp * block + x * BATCH : comp * block + (x + 1) * BATCH, :]
                        for x in range(GRID)
                    ]
                )
                for k in range(GRID):
                    at = comp * block + flip(comp, k) * BATCH
                    spec[half, at : at + BATCH, :] = lines[k]
            wave_y = jnp.broadcast_to(table[half, GRID : GRID + 1, :], (BATCH, LANES))
            wave_z = jnp.broadcast_to(table[half, GRID + 1 : GRID + 2, :], (BATCH, LANES))
            for k in range(GRID):
                wave_x = waves[k]
                inv_sq = jnp.broadcast_to(table[half, k : k + 1, :], (BATCH, LANES))
                s = [
                    spec[half, comp * block + k * BATCH : comp * block + (k + 1) * BATCH, :]
                    for comp in range(6)
                ]
                comp_a = s[0] * wave_x + s[5] * wave_y + s[4] * wave_z
                comp_b = s[5] * wave_x + s[1] * wave_y + s[3] * wave_z
                comp_c = s[4] * wave_x + s[3] * wave_y + s[2] * wave_z
                along = (wave_x * comp_a + wave_y * comp_b + wave_z * comp_c) * (
                    inv_sq * coupling
                )
                scale = inv_sq * scale_cell
                vec_a = (comp_a - along * wave_x) * scale
                vec_b = (comp_b - along * wave_y) * scale
                vec_c = (comp_c - along * wave_z) * scale
                mapped = (
                    wave_x * vec_a,
                    wave_y * vec_b,
                    wave_z * vec_c,
                    0.5 * (wave_y * vec_c + wave_z * vec_b),
                    0.5 * (wave_x * vec_c + wave_z * vec_a),
                    0.5 * (wave_x * vec_b + wave_y * vec_a),
                )
                for comp in range(6):
                    at = comp * block + flip(comp, k) * BATCH
                    work[half, at : at + BATCH, :] = mapped[comp]
            return inner

        for half in range(2):
            spectral(half, 0)
            for comp in range(6):
                lines = hartley(
                    [
                        work[half, comp * block + x * BATCH : comp * block + (x + 1) * BATCH, :]
                        for x in range(GRID)
                    ]
                )
                for pair in range(GRID // 2):
                    value = jnp.concatenate([lines[2 * pair], lines[2 * pair + 1]], axis=0)
                    split_store(comp, pair, half, value)
        plane_product(update_field)
        return carry

    lax.fori_loop(0, most, sweep, 0)

    acc[...] = jnp.zeros_like(acc)

    def finish(pair, carry):
        for half in range(2):
            load, volume, mu, dev, squared = trial(half, pair)
            base = load(9)
            trial_eq = jnp.sqrt(squared)
            excess = trial_eq - load(12)
            over = jnp.maximum(excess, 0.0)
            inc = increments(load, mu, over)
            inv_eq = 1.0 / jnp.maximum(trial_eq, base)
            lost = 3.0 * mu * inc * inv_eq
            shrink = 1.0 - lost
            pressure = load(8) * volume
            grow = 1.5 * inc * inv_eq
            for comp in range(6):
                work[half, pl.ds(comp * block + pair * 16, 16), :] = load(comp) + grow * dev[comp]
            spec[half, pl.ds(pair * 16, 16), :] = load(6) + inc
            rate = load(11)
            slope = load(13) * rate * jnp.exp(-rate * inc) + SLOPE
            corr = jnp.where(excess > 0.0, 3.0 * mu / (3.0 * mu + slope) - lost, 0.0)
            weight = 3.0 * mu * corr * (inv_eq * inv_eq)
            terms = [shrink * part for part in dev]
            terms = [term + pressure for term in terms[:3]] + terms[3:]
            terms.append(load(8))
            terms.append(2.0 * mu * shrink)
            for c in range(6):
                scaled = weight * dev[c]
                for d in range(c, 6):
                    terms.append(scaled * dev[d])
            for at, term in enumerate(terms):
                acc[at] = acc[at] + (term[:BATCH] + term[BATCH:])
        return carry

    lax.fori_loop(0, GRID // 2, finish, 0)

    lane_of = lax.broadcasted_iota(jnp.int32, (BATCH, LANES), 1)
    out = jnp.zeros((BATCH, LANES), jnp.float32)
    for at in range(SUMS):
        out = jnp.where(lane_of == at, jnp.sum(acc[at], axis=1, keepdims=True), out)
    sums[...] = out * (1.0 / (GRID * PLANE))

    ahead = max(begin - first, 0)
    if begin:
        for at in range(ahead):
            after[at] = other[at]
    for slot in range(min(BATCH, total - begin)):
        alone = begin == 0 and slot < first
        target = other if alone else after
        here = slot if alone else begin + slot - first
        for half in range(2):
            for part in range(2):
                near = part * 16 + half
                for row in range(7):
                    source, from_row = (work, row) if row < 6 else (spec, 0)
                    at = (0 if alone else P_ROWS) + row * LINES + near
                    target[here, pl.ds(at, 8, stride=2), :] = source[
                        half, pl.ds(from_row * block + part * 64 + slot, 8, stride=BATCH), :
                    ]
                if not alone:
                    for row in range(5):
                        target[here, pl.ds(row * LINES + near, 8, stride=2), :] = rec[
                            half, pl.ds((7 + row) * block + part * 64 + slot, 8, stride=BATCH), :
                        ]


def merge_kernel(
    elems,
    points,
    first,
    order,
    rem,
    s_head,
    got_p,
    got_s,
    shear,
    bulk,
    base,
    sat,
    rate,
    new_state,
    new_props,
    cells,
    s_out,
    p_out,
    in_sem,
    out_sem,
):
    total = elems * points
    moving = order[total]
    rows = LINES * points

    def arrival(slot):
        late = slot - first
        return pltpu.make_async_copy(rem.at[late], cells.at[late], in_sem.at[late])

    def leaving(e_at):
        return (
            pltpu.make_async_copy(s_out.at[e_at], new_state.at[e_at], out_sem.at[e_at, 0]),
            pltpu.make_async_copy(p_out.at[e_at], new_props.at[e_at], out_sem.at[e_at, 1]),
        )

    def put(target, cell, count, load):
        for row in range(count):
            for part in range(0, LINES, 8):
                at = row * rows + part * points + cell % points
                target[cell // points, pl.ds(at, 8, stride=points), :] = load(row * LINES + part)

    @pl.loop(first, total)
    def _(slot):
        arrival(slot).start()

    @pl.loop(0, elems)
    def _(e_at):
        for row, source in enumerate((shear, bulk, base, sat, rate)):
            p_out[e_at, pl.ds(row * rows, rows), :] = source[
                pl.ds(pl.multiple_of(e_at * rows, rows), rows), :
            ]

    @pl.loop(0, first)
    def _(slot):
        cell = order[slot]

        @pl.when(slot < moving)
        def _():
            put(p_out, cell, 5, lambda at: got_p[slot, at : at + 8, :])
            put(s_out, cell, 7, lambda at: got_s[slot, at : at + 8, :])

        @pl.when(slot >= moving)
        def _():
            put(s_out, cell, 7, lambda at: s_head[slot, at : at + 8, :])

    @pl.loop(0, elems)
    def _(e_at):
        @pl.loop(0, points)
        def _(g_at):
            cell = e_at * points + g_at
            slot = order[total + 1 + cell]
            late = jnp.maximum(slot - first, 0)

            @pl.when(slot >= first)
            def _():
                arrival(jnp.maximum(slot, first)).wait()
                put(s_out, cell, 7, lambda at: cells[late, P_ROWS + at : P_ROWS + at + 8, :])

            @pl.when((slot >= first) & (slot < moving))
            def _():
                put(p_out, cell, 5, lambda at: cells[late, at : at + 8, :])

        for copy in leaving(e_at):
            copy.start()

    @pl.loop(0, elems)
    def _(e_at):
        for copy in leaving(e_at):
            copy.wait()


def element_terms(table_part, sums, points):
    elems = sums.shape[0] // points
    weights = np.array([1.0, 1.0, 1.0, 2.0, 2.0, 2.0], np.float32)
    stress = sums[:, 0:6]
    block = np.outer([1.0, 1.0, 1.0, 0.0, 0.0, 0.0], [1.0, 1.0, 1.0, 0.0, 0.0, 0.0])
    spread = np.zeros((23, 36), np.float32)
    spread[0] = block.reshape(36)
    spread[1] = (np.eye(6) - block / 3.0).reshape(36)
    at = 2
    for c in range(6):
        for d in range(c, 6):
            spread[at, 6 * c + d] = -weights[d]
            spread[at, 6 * d + c] = -weights[c]
            at += 1
    tangent = jnp.dot(sums[:, 6:SUMS], spread, precision=top_precision)
    stress_part = stress.reshape(elems, points, 6)
    force = (
        jnp.einsum("egc,gcn->en", stress_part * weights, table_part, precision=top_precision)
        / GAUSS
    )
    scaled = tangent.reshape(elems, points, 6, 6) * weights[None, None, :, None]
    stiff = (
        jnp.einsum(
            "gcn,egcd,gdm->enm", table_part, scaled, table_part, precision=top_precision
        ).reshape(elems, 576)
        / GAUSS
    )
    return stress_part, force, stiff


VMEM = pl.BlockSpec(memory_space=pltpu.VMEM)
SMEM = pl.BlockSpec(memory_space=pltpu.SMEM)
ANY = pl.BlockSpec(memory_space=pl.ANY)
GRANT = 60 * 2**20
MERGE_GRANT = 24 * 2**20


def shape(*dims, dtype=jnp.float32):
    return jax.ShapeDtypeStruct(dims, dtype)


def local(
    elem_disp,
    plastic_strain,
    hardening_var,
    shear_mod,
    bulk_mod,
    yield_stress,
    sat_stress,
    sat_rate,
    fft_iters,
    rm_iters,
    move_flag,
):
    elems, points = plastic_strain.shape[:2]
    voxels = plastic_strain.shape[3]
    total = elems * points
    group = min(BATCH, total)
    first = max(1, total * EARLY // 16)
    devices = lax.axis_size("cell")
    route = [((i - devices // 2) % devices, i) for i in range(devices)]

    params = pltpu.CompilerParams(vmem_limit_bytes=GRANT)
    bmat = jnp.asarray(strain_table())

    def flat(array):
        lead = array.shape[2:-1]
        tiles = array.reshape(elems, points, *lead, LINES, LANES)
        return jnp.moveaxis(tiles, 1, -2).reshape(-1, LANES)

    def whole(lines, lead):
        tiles = lines.reshape(elems, lead, LINES, points, LANES)
        return jnp.moveaxis(tiles, 3, 1).reshape(elems, points, lead, voxels)

    props = [flat(a) for a in (shear_mod, bulk_mod, yield_stress, sat_stress, sat_rate)]
    hard, plastic = flat(hardening_var), flat(plastic_strain)
    order, p_head = pl.pallas_call(
        functools.partial(pack_kernel, elems, points, first),
        out_shape=(shape(2 * total + 1, dtype=jnp.int32), shape(first, P_ROWS, LANES)),
        in_specs=[SMEM] + [VMEM] * 5,
        out_specs=(SMEM, VMEM),
        compiler_params=params,
        name="pack",
    )(move_flag, *props)

    got_p = lax.ppermute(p_head, "cell", route)

    high, low, table, waves = cas_tables()
    table = table.reshape(24, 2, LANES).transpose(1, 0, 2)
    block = GRID * BATCH
    disp = elem_disp.reshape(elems, 1, elem_disp.shape[1])

    def solve(begin, count, other=None):
        late = shape(count, ROWS, LANES)
        alone = () if begin else (shape(first, S_ROWS, LANES),)
        return pl.pallas_call(
            functools.partial(solve_kernel, elems, points, begin, first, waves),
            out_shape=alone + (late, shape(BATCH, LANES)),
            in_specs=[SMEM] * 3 + [VMEM] * (13 if begin else 12),
            out_specs=(VMEM,) * (len(alone) + 2),
            scratch_shapes=[
                pltpu.VMEM((2, 15 * block, LANES), jnp.float32),
                pltpu.VMEM((2, 6 * block, LANES), jnp.float32),
                pltpu.VMEM((2, 6 * block, LANES), jnp.float32),
                pltpu.VMEM((2, 6 * block, LANES), jnp.float32),
                pltpu.VMEM((2 * 6 * block, PLANE), jnp.bfloat16),
                pltpu.VMEM((SUMS, BATCH, LANES), jnp.float32),
            ],
            compiler_params=params,
            cost_estimate=pl.CostEstimate(
                flops=20 * 10**9, bytes_accessed=8 * 10**6, transcendentals=0
            ),
            name="solve",
        )(
            order,
            fft_iters,
            rm_iters,
            disp,
            bmat,
            plastic,
            hard,
            *props,
            high,
            low,
            table,
            *(() if other is None else (other,)),
        )

    s_head, rem, sums = solve(0, group - first)
    got_s = lax.ppermute(s_head, "cell", route)
    if total > group:
        rem, more = solve(group, total - first, rem)
        sums = jnp.concatenate([sums, more], axis=0)

    slots = order[:total]
    place = (slots[None, :] == jnp.arange(total)[:, None]).astype(jnp.float32)
    sums = jnp.dot(place, sums[:total], precision=top_precision)
    table_part = lax.dynamic_slice_in_dim(bmat, lax.axis_index("sec") * points, points, 0)
    stress, force_part, stiff_part = element_terms(table_part, sums, points)
    sections = lax.axis_size("sec")
    force, stiff = force_part, stiff_part
    for step in range(1, sections):
        ring = [((i - step) % sections, i) for i in range(sections)]
        force = force + lax.ppermute(force_part, "sec", ring)
        stiff = stiff + lax.ppermute(stiff_part, "sec", ring)
    rem, force, stiff, stress = lax.optimization_barrier((rem, force, stiff, stress))

    def branch(count):
        def run(cells):
            if count == 0:
                return cells
            got = lax.ppermute(cells[:count], "cell", route)
            return lax.dynamic_update_slice_in_dim(cells, got, 0, 0)

        return run

    extra = jnp.clip(
        jnp.sum((move_flag > 0).astype(jnp.int32)) - first, 0, total - first
    )
    rem = lax.switch(extra, [branch(c) for c in range(total - first + 1)], rem)

    new_state, new_props = pl.pallas_call(
        functools.partial(merge_kernel, elems, points, first),
        out_shape=(
            shape(elems, 7 * LINES * points, LANES),
            shape(elems, 5 * LINES * points, LANES),
        ),
        in_specs=[SMEM, ANY] + [VMEM] * 8,
        out_specs=(ANY, ANY),
        scratch_shapes=[
            pltpu.VMEM((total - first, ROWS, LANES), jnp.float32),
            pltpu.VMEM((elems, 7 * LINES * points, LANES), jnp.float32),
            pltpu.VMEM((elems, 5 * LINES * points, LANES), jnp.float32),
            pltpu.SemaphoreType.DMA((total - first,)),
            pltpu.SemaphoreType.DMA((elems, 2)),
        ],
        compiler_params=pltpu.CompilerParams(vmem_limit_bytes=MERGE_GRANT),
        name="merge",
    )(order, rem, s_head, got_p, got_s, *props)
    return force, stiff, stress, whole(new_state, 7), whole(new_props, 5)


def solution(mesh):
    in_specs = (
        P("cell", None),
        P("cell", "sec", None, None),
        P("cell", "sec", None),
        P("cell", "sec", None),
        P("cell", "sec", None),
        P("cell", "sec", None),
        P("cell", "sec", None),
        P("cell", "sec", None),
        P("cell", "sec"),
        P("cell", "sec"),
        P("cell", "sec"),
    )
    out_specs = (
        P("cell", None),
        P("cell", None),
        P("cell", "sec", None),
        P("cell", "sec", None, None),
        P("cell", "sec", None, None),
    )

    return jax.shard_map(local, mesh=mesh, in_specs=in_specs, out_specs=out_specs, check_vma=False)
```
